32 devices in a mesh: space: 8 (over y, x, core), chan: 4 (over z).
Axes of the slice: x: 2, y: 2, z: 4, core: 2. Of those that a mesh axis runs over, the one named last changes fastest.
Arguments:
- points: bfloat16 [256, 8, 16384], P('chan', 'space'), may hold values from -6 to 6
- point_cell: int32 [8, 16384], P('space'), may hold values from 0 to 4096, as said below
- conv_weight: bfloat16 [27, 256, 256], P(None, 'chan'), may hold values from -0.109375 to 0.109375
- conv_bias: bfloat16 [256], P('chan'), may hold values from -3 to 3
- neighbors: int32 [64, 27], P('space'), may hold values from -1 to 23, as said below
Outputs:
- voxel_out: bfloat16 [256, 32768], P('chan', 'space')
- point_out: bfloat16 [256, 8, 16384], P('chan', 'space')
The draws below stay inside these ranges and needn't reach their ends.
Inputs may be any that keep to these rules, and one draw needn't show every extreme that they name: `point_cell`: in each aligned block of 2048 slots from one sender the live slots (cell below 4096) come first; in every draw some owner receives 2048 live slots from every sender. `neighbors`: entry 13 is the block's own slot 8 + b; blocks of one owner lie on a 4 x (4) grid of a strip, strips of owners d and d+1 adjacent.
All inputs are finite; a program needn't handle non-finite values.
Results may differ from the reference program's by a relative error of at most 0.01.
Values may be sent and summed in bfloat16 or wider, within the bound.
A program may use at most 128 MiB of HBM per device.

```python
import jax
import jax.numpy as jnp
from jax import lax

C = 256
B_DEV = 8
PTS_DEV = 16384
N_SPACE = 8
N_CHAN = 4


def draw_point_cell(key, part):
    slot_cap = PTS_DEV // N_SPACE
    keys = jax.random.split(key, 5)
    levels = jnp.array([1, 1, 1, 2, 4], dtype=jnp.int32)
    owner_weight = levels[jax.random.randint(keys[0], (N_SPACE,), 0, 5)]
    busiest = jax.random.randint(keys[1], (), 0, N_SPACE)
    jitter = jax.random.randint(keys[2], (N_SPACE, N_SPACE), 0, slot_cap // 8 + 1)
    live_count = jnp.clip(slot_cap * owner_weight[:, None] // 4 - jitter, 0, slot_cap)
    owner_ids = jnp.arange(N_SPACE, dtype=jnp.int32)[:, None]
    live_count = jnp.where(owner_ids == busiest, slot_cap, live_count)
    block_id = jax.random.randint(keys[3], (N_SPACE, N_SPACE, slot_cap), 0, B_DEV)
    within = jax.random.randint(keys[4], (N_SPACE, N_SPACE, slot_cap), 0, 512)
    slot_ids = jnp.arange(slot_cap, dtype=jnp.int32)[None, None, :]
    cell_ids = jnp.where(slot_ids < live_count[:, :, None], block_id * 512 + within, B_DEV * 512)
    return cell_ids.reshape(N_SPACE, PTS_DEV).astype(jnp.int32)


def draw_neighbors(key, part):
    half_side = B_DEV // 2
    keys = jax.random.split(key, N_SPACE)
    orders = jax.vmap(lambda single: jax.random.permutation(single, 2 * B_DEV))(keys)
    places = orders[:, :B_DEV].astype(jnp.int32)
    coord_y = places // half_side
    coord_z = places % half_side
    owner_ids = jnp.arange(N_SPACE, dtype=jnp.int32)
    slot_ids = jnp.arange(B_DEV, dtype=jnp.int32)
    entries = []
    for shift_x in (-1, 0, 1):
        for shift_y in (-1, 0, 1):
            for shift_z in (-1, 0, 1):
                target_owner = owner_ids + shift_x
                owner_valid = (target_owner >= 0) & (target_owner < N_SPACE)
                clipped = jnp.clip(target_owner, 0, N_SPACE - 1)
                target_y = coord_y + shift_y
                target_z = coord_z + shift_z
                inside = (target_y >= 0) & (target_y < 4) & (target_z >= 0) & (target_z < half_side)
                target_place = target_y * half_side + target_z
                others = places[clipped]
                matches = others[:, None, :] == target_place[:, :, None]
                found = jnp.any(matches, axis=2)
                found_slot = jnp.sum(jnp.where(matches, slot_ids[None, None, :], 0), axis=2)
                entry = jnp.where(owner_valid[:, None] & inside & found, (shift_x + 1) * B_DEV + found_slot, -1)
                entries.append(entry)
    return jnp.stack(entries, 2).reshape(N_SPACE * B_DEV, 27).astype(jnp.int32)


def strengthened(values, key, source, target, shards_of, factor):
    owner, partner = [(jnp.arange(values.shape[dim]) // (values.shape[dim] // shards_of)).reshape([-1 if axis == dim else 1 for axis in range(values.ndim)]) for dim in (source, target)]
    chosen = jax.random.permutation(key, shards_of)[partner]
    strong = (owner == chosen) | (owner == (partner + shards_of // 2) % shards_of)
    return jnp.where(strong, factor * values, values)


def block_levels(rng, shape, cuts, least, top_value):
    level = 1.0
    for position, parts in cuts:
        steps = jax.random.uniform(jax.random.fold_in(jax.random.fold_in(rng, 6), position), (parts,), jnp.float32, least / len(cuts), top_value / len(cuts))
        level = level * jnp.repeat(jnp.exp(steps), shape[position] // parts).reshape((-1,) + (1,) * (len(shape) - 1 - position))
    return level


def bell_draw(own_key, extent, deviation, most, cuts=(), held_as=jnp.bfloat16):
    values = deviation * jax.random.normal(own_key, extent, jnp.float32)
    if cuts:
        values = values * block_levels(own_key, extent, cuts, -0.22, 0.18)
    return jnp.clip(values, -most, most).astype(held_as)


def gaussian_with(rng, shape, deviation, limit, cuts, heavy, kind=jnp.bfloat16):
    values = deviation * jax.random.normal(rng, shape, jnp.float32)
    if cuts:
        values = values * block_levels(rng, shape, cuts, -0.22, 0.18)
    return jnp.clip(strengthened(values, jax.random.fold_in(rng, 3), *heavy), -limit, limit).astype(kind)


def setup_inputs(seed: int = 0) -> dict:
    key_list = jax.random.split(jax.random.key(seed), 6)
    points = bell_draw(key_list[0], (C, N_SPACE, PTS_DEV), 1.0, 6.0, ((0, 4), (1, 8)))
    point_cell = draw_point_cell(jax.random.fold_in(key_list[5], 71), 0)
    conv_weight = gaussian_with(key_list[2], (27, C, C), (27 * C) ** -0.5, 0.109375, ((1, 4),), (1, 2, 4, 2.0))
    conv_bias = bell_draw(key_list[3], (C,), 0.5, 3.0, ((0, 4),))
    neighbors = draw_neighbors(jax.random.fold_in(key_list[5], 71), 0)
    return {"points": points, "point_cell": point_cell, "conv_weight": conv_weight, "conv_bias": conv_bias, "neighbors": neighbors}


def assemble(source, lookup):
    spare = source.shape[1] - 1
    picked = jnp.where(lookup < 0, spare, lookup).astype(jnp.int32)
    nearby = jnp.take(source, picked.reshape(-1), axis=1)
    width_here = source.shape[0]
    block_count = lookup.shape[0]
    nearby = nearby.reshape(width_here, block_count, 3, 3, 3, 8, 8, 8)
    nearby = jnp.transpose(nearby, (0, 1, 2, 5, 3, 6, 4, 7)).reshape(width_here, block_count, 24, 24, 24)
    return nearby[:, :, 7:17, 7:17, 7:17]


def columns(padded):
    width_here = padded.shape[0]
    block_count = padded.shape[1]
    pieces = []
    for shift_x in range(3):
        for shift_y in range(3):
            for shift_z in range(3):
                window = padded[:, :, shift_x:shift_x + 8, shift_y:shift_y + 8, shift_z:shift_z + 8]
                pieces.append(window.reshape(width_here, block_count * 512))
    return jnp.stack(pieces, 0).reshape(27 * width_here, block_count * 512)


def reference(points, point_cell, conv_weight, conv_bias, neighbors):
    slot_cap = PTS_DEV // N_SPACE
    width_all = points.shape[0]
    group_width = width_all // N_CHAN
    total_cells = B_DEV * 512

    def owner_pool(owner):
        arrived = lax.dynamic_slice_in_dim(points, owner * slot_cap, slot_cap, 2).reshape(width_all, N_SPACE * slot_cap)
        cell_ids = point_cell[owner]
        summed = jax.ops.segment_sum(arrived.astype(jnp.float32).T, cell_ids, num_segments=total_cells + 1)[:total_cells]
        tallies = jax.ops.segment_sum(jnp.ones(cell_ids.shape, jnp.float32), cell_ids, num_segments=total_cells + 1)[:total_cells]
        voxels = (summed / jnp.maximum(tallies, 1.0)[:, None]).astype(jnp.bfloat16)
        return voxels.T.reshape(width_all, B_DEV, 512), tallies

    voxels, tallies = lax.map(owner_pool, jnp.arange(N_SPACE, dtype=jnp.int32))
    border = jnp.zeros((1,) + voxels.shape[1:], voxels.dtype)
    widened = jnp.concatenate([border, voxels, border], 0)
    tables = neighbors.reshape(N_SPACE, B_DEV, 27)
    empty_block = jnp.zeros((width_all, 1, 512), voxels.dtype)
    bias_full = conv_bias.astype(jnp.float32)

    def owner_conv(owner):
        source = jnp.concatenate([widened[owner], widened[owner + 1], widened[owner + 2], empty_block], 1)
        padded = assemble(source, tables[owner])
        active = jnp.where(tallies[owner] > 0.0, 1.0, 0.0).astype(jnp.float32)
        total = jnp.zeros((width_all, total_cells), jnp.float32)
        for group in range(N_CHAN):
            low = group * group_width
            w_group = conv_weight[:, low:low + group_width, :].reshape(27 * group_width, width_all)
            stacked = columns(padded[low:low + group_width])
            partial_sum = jnp.dot(w_group.T, stacked, preferred_element_type=jnp.float32).astype(jnp.bfloat16)
            partial_sum = lax.optimization_barrier(partial_sum)
            total = total + partial_sum.astype(jnp.float32)
        result = (jnp.maximum(total + bias_full[:, None], 0.0) * active[None, :]).astype(jnp.bfloat16)
        extended = jnp.concatenate([result, jnp.zeros((width_all, 1), result.dtype)], 1)
        picked = jnp.take(extended, point_cell[owner], axis=1).reshape(width_all, N_SPACE, slot_cap)
        return result, picked

    results, picked = lax.map(owner_conv, jnp.arange(N_SPACE, dtype=jnp.int32))
    voxel_out = jnp.transpose(results, (1, 0, 2)).reshape(width_all, N_SPACE * total_cells)
    returned = jnp.transpose(picked, (1, 2, 0, 3)).reshape(width_all, N_SPACE, PTS_DEV)
    point_out = (points.astype(jnp.float32) + returned.astype(jnp.float32)).astype(jnp.bfloat16)
    return (voxel_out, point_out)
```

```python
import functools

import jax
import jax.numpy as jnp
from jax import lax
from jax.experimental import pallas as pl
from jax.experimental.pallas import tpu as pltpu
from jax.sharding import PartitionSpec as P

VMEM_LIMIT = 60 * 1024 * 1024
CELLS = 512
MESH = pl.DeviceIdType.MESH
ROWS = 1008


def params():
    return pltpu.CompilerParams(vmem_limit_bytes=VMEM_LIMIT)


def greet(axis, count):
    me = lax.axis_index(axis)
    barrier = pltpu.get_barrier_semaphore()

    def signal(t, carry):
        pl.semaphore_signal(barrier, inc=1, device_id={axis: lax.rem(me + t, count)}, device_id_type=MESH)
        return carry

    lax.fori_loop(1, count, signal, 0)
    pl.semaphore_wait(barrier, count - 1)
    return me


def remote_params(collective_id):
    return pltpu.CompilerParams(
        vmem_limit_bytes=VMEM_LIMIT, collective_id=collective_id, has_side_effects=True
    )


def pool_kernel(groups, low_cells, owners, x_ref, id_ref, count_ref, o_ref, held, acc_ref, send_sem, recv_sem, own_sem):
    width, rows = held.shape[1], held.shape[2]
    me = greet("space", owners)

    def chunk(d):
        return x_ref.at[:, pl.ds(pl.multiple_of(d * rows, rows), rows)]

    def copy(t):
        peer = lax.rem(me + t, owners)
        return pltpu.make_async_remote_copy(
            src_ref=chunk(peer),
            dst_ref=held.at[t],
            send_sem=send_sem.at[t],
            recv_sem=recv_sem.at[t],
            device_id={"space": peer},
            device_id_type=MESH,
        )

    def send(t, carry):
        copy(t).start()
        return carry

    lax.fori_loop(1, owners, send, 0)
    own = pltpu.make_async_copy(chunk(me), held.at[0], own_sem)
    own.start()
    acc_ref[...] = jnp.zeros_like(acc_ref)
    spots = lax.broadcasted_iota(jnp.int32, (low_cells, rows), 0)

    def add_chunk(t):
        ids = id_ref[lax.rem(me + owners - t, owners)]
        high = ids // low_cells
        low = ids % low_cells
        x = held[t]
        zero = jnp.zeros_like(x)
        masked = jnp.concatenate(
            [jnp.where(jnp.broadcast_to(high, x.shape) == g, x, zero) for g in range(groups)], axis=0
        )
        onehot = jnp.where(spots == low, 1.0, 0.0).astype(jnp.bfloat16)
        acc_ref[...] += lax.dot_general(
            onehot, masked, (((1,), (1,)), ((), ())), preferred_element_type=jnp.float32
        )

    own.wait()
    add_chunk(0)

    def take(t, carry):
        copy(t).wait_recv()
        add_chunk(t)
        return carry

    lax.fori_loop(1, owners, take, 0)
    for g in range(groups):
        lanes = slice(g * width, (g + 1) * width)
        tally = jnp.maximum(count_ref[:, g : g + 1], 1.0)
        o_ref[:, lanes] = (acc_ref[:, lanes] / tally).astype(jnp.bfloat16)

    def close(t, carry):
        copy(t).wait_send()
        return carry

    lax.fori_loop(1, owners, close, 0)


def pool(points, ids, counts, groups, owners, cap):
    width = points.shape[0]
    low_cells = counts.shape[0] // groups
    by_group = counts.reshape(groups, low_cells).T
    vmem = pl.BlockSpec(memory_space=pltpu.VMEM)
    return pl.pallas_call(
        functools.partial(pool_kernel, groups, low_cells, owners),
        in_specs=[pl.BlockSpec(memory_space=pl.ANY), vmem, vmem],
        out_specs=vmem,
        out_shape=jax.ShapeDtypeStruct((low_cells, groups * width), jnp.bfloat16),
        scratch_shapes=[
            pltpu.VMEM((owners, width, cap), jnp.bfloat16),
            pltpu.VMEM((low_cells, groups * width), jnp.float32),
            pltpu.SemaphoreType.DMA((owners,)),
            pltpu.SemaphoreType.DMA((owners,)),
            pltpu.SemaphoreType.DMA,
        ],
        compiler_params=remote_params(0),
    )(points, ids.reshape(owners, 1, cap), by_group)


def exchange_kernel(axis, count, x_ref, o_ref, send_sem, recv_sem):
    me = greet(axis, count)

    def copy(t, landing):
        peer = lax.rem(me + t, count)
        return pltpu.make_async_remote_copy(
            src_ref=x_ref.at[peer],
            dst_ref=o_ref.at[landing],
            send_sem=send_sem.at[t],
            recv_sem=recv_sem.at[t],
            device_id={axis: peer},
            device_id_type=MESH,
        )

    def send(t, carry):
        copy(t, me).start()
        return carry

    def close(t, carry):
        copy(t, lax.rem(me + count - t, count)).wait_recv()
        copy(t, me).wait_send()
        return carry

    lax.fori_loop(1, count, send, 0)
    o_ref[me] = x_ref[me]
    lax.fori_loop(1, count, close, 0)


def exchange(x, axis, collective_id):
    count = lax.axis_size(axis)
    vmem = pl.BlockSpec(memory_space=pltpu.VMEM)
    return pl.pallas_call(
        functools.partial(exchange_kernel, axis, count),
        in_specs=[vmem],
        out_specs=vmem,
        out_shape=jax.ShapeDtypeStruct(x.shape, x.dtype),
        scratch_shapes=[pltpu.SemaphoreType.DMA((count,)), pltpu.SemaphoreType.DMA((count,))],
        compiler_params=remote_params(collective_id),
    )(x)


def margin_kernel(groups, share, nb_ref, left_ref, own_ref, right_ref, bias_ref, o_ref, v_ref, m_ref):
    blocks = groups * share
    width = bias_ref.shape[1]
    for a, ref in enumerate((left_ref, own_ref, right_ref)):
        for g in range(groups):
            for lb in range(share):
                part = ref[lb * CELLS : (lb + 1) * CELLS, g * width : (g + 1) * width]
                v_ref[a * blocks + g * share + lb] = part.astype(jnp.float32).reshape(64, 8, width)
    v_ref[3 * blocks] = jnp.zeros((64, 8, width), jnp.float32)
    bias = jnp.broadcast_to(bias_ref[...].astype(jnp.float32), (8, width))
    spans = (((0, 7),), tuple((t + 1, t) for t in range(8)), ((9, 0),))

    def one_block(b, carry):
        for dx in range(3):
            for dy in range(3):
                for dz in range(3):
                    slot = nb_ref[b, 9 * dx + 3 * dy + dz]
                    slot = jnp.where(slot < 0, 3 * blocks, slot)
                    for xd, xs in spans[dx]:
                        for yd, ys in spans[dy]:
                            row = 100 * xd + 10 * yd
                            if dz == 1:
                                m_ref[b, row + 1 : row + 9, :] = v_ref[slot, 8 * xs + ys]
                            else:
                                zd, zs = spans[dz][0]
                                m_ref[b, row + zd : row + zd + 1, :] = v_ref[slot, 8 * xs + ys, zs : zs + 1, :]
        m_ref[b, 1000:ROWS, :] = bias
        return carry

    lax.fori_loop(0, blocks, one_block, 0)
    for g in range(groups):
        for lb in range(share):
            o_ref[g, :, lb * width : (lb + 1) * width] = m_ref[g * share + lb].astype(jnp.bfloat16)


def build_margins(neighbors, left, own, right, bias, groups, share):
    width = bias.shape[1]
    blocks = groups * share
    vmem = pl.BlockSpec(memory_space=pltpu.VMEM)
    return pl.pallas_call(
        functools.partial(margin_kernel, groups, share),
        in_specs=[pl.BlockSpec(memory_space=pltpu.SMEM), vmem, vmem, vmem, vmem],
        out_specs=vmem,
        out_shape=jax.ShapeDtypeStruct((groups, ROWS, share * width), jnp.bfloat16),
        scratch_shapes=[
            pltpu.VMEM((3 * blocks + 1, 64, 8, width), jnp.float32),
            pltpu.VMEM((blocks, ROWS, width), jnp.float32),
        ],
        compiler_params=params(),
    )(neighbors, left, own, right, bias)


def conv_kernel(share, m_ref, w_ref, act_ref, o_ref, f_ref, q_ref):
    halves, groups, _, part, outs = w_ref.shape
    width = halves * part
    wide = groups * width
    for lb in range(share):
        for g in range(groups):
            f_ref[lb, :, g * width : (g + 1) * width] = m_ref[g, :, lb * width : (lb + 1) * width].astype(jnp.float32)
    for k in range(3):
        for lb in range(share):
            for p in range(6):
                for y in range(10):
                    near = 100 * p + 10 * y + k
                    far = near + 400
                    q_ref[k, lb, p, y] = jnp.concatenate(
                        [f_ref[lb, near : near + 8, :], f_ref[lb, far : far + 8, :]], axis=0
                    ).astype(jnp.bfloat16)
    bias = f_ref[0, 1000:1001, :]
    for lb in range(share):
        total = None
        for k in range(3):
            windows, weights = [], []
            for i in range(3):
                for j in range(3):
                    windows.append(q_ref[k, lb, i : i + 4, j : j + 8].reshape(CELLS, wide))
                    for g in range(groups):
                        for half in range(halves):
                            weights.append(w_ref[half, g, 9 * i + 3 * j + k])
            term = jnp.dot(
                jnp.concatenate(windows, axis=1),
                jnp.concatenate(weights, axis=0),
                preferred_element_type=jnp.float32,
            )
            total = term if total is None else total + term
        total = jnp.maximum(total + bias, 0.0).reshape(4, 8, 2, 8, outs)
        for h in range(2):
            half = total[:, :, h].reshape(256, outs).T
            seg = slice(lb * CELLS + h * 256, lb * CELLS + (h + 1) * 256)
            o_ref[:, seg] = (half * act_ref[:, seg]).astype(jnp.bfloat16)


def convolve(spread, weight_all, active, share):
    halves, groups, _, part, outs = weight_all.shape
    vmem = pl.BlockSpec(memory_space=pltpu.VMEM)
    return pl.pallas_call(
        functools.partial(conv_kernel, share),
        in_specs=[vmem] * 3,
        out_specs=vmem,
        out_shape=jax.ShapeDtypeStruct((outs, share * CELLS), jnp.bfloat16),
        scratch_shapes=[
            pltpu.VMEM((share, ROWS, groups * halves * part), jnp.float32),
            pltpu.VMEM((3, share, 6, 10, 16, groups * halves * part), jnp.bfloat16),
        ],
        compiler_params=params(),
    )(spread, weight_all, active)


def return_kernel(groups, owners, v_ref, id_ref, p_ref, o_ref, found_ref, held, send_sem, recv_sem):
    width, low_cells = v_ref.shape[0] // groups, v_ref.shape[1]
    rows = id_ref.shape[2]
    me = greet("space", owners)
    spots = lax.broadcasted_iota(jnp.int32, (low_cells, rows), 0)

    def copy(t):
        return pltpu.make_async_remote_copy(
            src_ref=found_ref.at[t],
            dst_ref=held.at[t],
            send_sem=send_sem.at[t],
            recv_sem=recv_sem.at[t],
            device_id={"space": lax.rem(me + t, owners)},
            device_id_type=MESH,
        )

    def pick(s):
        ids = id_ref[s]
        high = ids // low_cells
        low = ids % low_cells
        onehot = jnp.where(spots == low, 1.0, 0.0).astype(jnp.bfloat16)
        found = jnp.dot(v_ref[...], onehot, preferred_element_type=jnp.float32)
        total = jnp.zeros((width, rows), jnp.float32)
        for g in range(groups):
            total = jnp.where(jnp.broadcast_to(high, total.shape) == g, found[g * width : (g + 1) * width], total)
        return total

    def add(d, values):
        at = pl.ds(pl.multiple_of(d * rows, rows), rows)
        o_ref[:, at] = (p_ref[:, at].astype(jnp.float32) + values).astype(jnp.bfloat16)

    def send(t, carry):
        found_ref[t] = pick(lax.rem(me + t, owners)).astype(jnp.bfloat16)
        copy(t).start()
        return carry

    def take(t, carry):
        copy(t).wait_recv()
        add(lax.rem(me + owners - t, owners), held[t].astype(jnp.float32))
        return carry

    def close(t, carry):
        copy(t).wait_send()
        return carry

    lax.fori_loop(1, owners, send, 0)
    add(me, pick(me))
    lax.fori_loop(1, owners, take, 0)
    lax.fori_loop(1, owners, close, 0)


def give_back(parts, ids, points, owners, cap):
    groups, width, low_cells = parts.shape
    vmem = pl.BlockSpec(memory_space=pltpu.VMEM)
    return pl.pallas_call(
        functools.partial(return_kernel, groups, owners),
        in_specs=[vmem] * 3,
        out_specs=vmem,
        out_shape=jax.ShapeDtypeStruct(points.shape, jnp.bfloat16),
        scratch_shapes=[
            pltpu.VMEM((owners, width, cap), jnp.bfloat16),
            pltpu.VMEM((owners, width, cap), jnp.bfloat16),
            pltpu.SemaphoreType.DMA((owners,)),
            pltpu.SemaphoreType.DMA((owners,)),
        ],
        compiler_params=remote_params(3),
    )(parts.reshape(groups * width, low_cells), ids.reshape(owners, 1, cap), points)


def flip(me, mask):
    value = me
    for bit in (1, 2, 4):
        if mask & bit:
            value = value + bit - 2 * bit * (lax.rem(me // bit, 2))
    return value


def finish_kernel(
    share, owners, m_ref, w_ref, act_ref, id_ref, vox_ref, pick_ref,
    f_ref, q_ref, fin_ref, tab_ref, sid_ref,
    id_send, id_recv, back_send, back_recv, tab_send, tab_recv,
):
    halves, groups, _, part, outs = w_ref.shape
    width = halves * part
    wide = groups * width
    split = wide // 2
    rows = id_ref.shape[2]
    me = lax.axis_index("space")
    row = lax.axis_index("chan")
    barrier = pltpu.get_barrier_semaphore()
    for r in range(1, owners):
        pl.semaphore_signal(barrier, inc=1, device_id={"space": flip(me, r)}, device_id_type=MESH)
    for t in range(1, groups):
        pl.semaphore_signal(barrier, inc=1, device_id={"chan": lax.rem(row + t, groups)}, device_id_type=MESH)
    pl.semaphore_wait(barrier, owners + groups - 2)

    def id_copy(r):
        peer = flip(me, r)
        return pltpu.make_async_remote_copy(
            src_ref=id_ref.at[peer],
            dst_ref=sid_ref.at[r],
            send_sem=id_send.at[r],
            recv_sem=id_recv.at[r],
            device_id={"space": peer},
            device_id_type=MESH,
        )

    for r in range(1, owners):
        id_copy(r).start()
    sid_ref[0] = id_ref[me]

    def lane_rows(index):
        return pl.ds(pl.multiple_of(index * width, width), width)

    def back(lb, t, landing):
        peer = lax.rem(row + t, groups)
        return pltpu.make_async_remote_copy(
            src_ref=fin_ref.at[lb, lane_rows(peer)],
            dst_ref=tab_ref.at[0, lb, lane_rows(landing)],
            send_sem=back_send.at[lb, t],
            recv_sem=back_recv.at[lb, t],
            device_id={"chan": peer},
            device_id_type=MESH,
        )

    edges = (
        (0, 1, 1, 0, wide),
        (0, 2, 2, 0, wide),
        (0, 4, 4, 0, wide),
        (2, 3, 1, 0, wide),
        (4, 5, 1, 0, wide),
        (2, 6, 4, 0, split),
        (4, 6, 2, split, wide),
        (6, 7, 1, 0, wide),
    )

    def edge(lb, e):
        source, target, mask, low, high = edges[e]
        return pltpu.make_async_remote_copy(
            src_ref=tab_ref.at[source, lb, low:high],
            dst_ref=tab_ref.at[target, lb, low:high],
            send_sem=tab_send.at[lb, e],
            recv_sem=tab_recv.at[lb, e],
            device_id={"space": flip(me, mask)},
            device_id_type=MESH,
        )

    for g in range(groups):
        for lb in range(share):
            f_ref[lb, :, g * width : (g + 1) * width] = m_ref[g, :, lb * width : (lb + 1) * width].astype(jnp.float32)
    bias = f_ref[0, 1000:1001, :]

    def conv(lb):
        for k in range(3):
            for p in range(6):
                for y in range(10):
                    near = 100 * p + 10 * y + k
                    far = near + 400
                    q_ref[k, p, y] = jnp.concatenate(
                        [f_ref[lb, near : near + 8, :], f_ref[lb, far : far + 8, :]], axis=0
                    ).astype(jnp.bfloat16)
        total = None
        for k in range(3):
            windows, weights = [], []
            for i in range(3):
                for j in range(3):
                    windows.append(q_ref[k, i : i + 4, j : j + 8].reshape(CELLS, wide))
                    for g in range(groups):
                        for half in range(halves):
                            weights.append(w_ref[half, g, 9 * i + 3 * j + k])
            term = jnp.dot(
                jnp.concatenate(windows, axis=1),
                jnp.concatenate(weights, axis=0),
                preferred_element_type=jnp.float32,
            )
            total = term if total is None else total + term
        total = jnp.maximum(total + bias, 0.0).reshape(4, 8, 2, 8, outs)
        for h in range(2):
            half = total[:, :, h].reshape(256, outs).T
            seg = slice(lb * CELLS + h * 256, lb * CELLS + (h + 1) * 256)
            fin_ref[lb, :, h * 256 : (h + 1) * 256] = (half * act_ref[:, seg]).astype(jnp.bfloat16)
        for t in range(1, groups):
            back(lb, t, row).start()
        tab_ref[0, lb, lane_rows(row)] = fin_ref[lb, lane_rows(row)]

    def gather_back(lb):
        for t in range(1, groups):
            back(lb, t, lax.rem(row + groups - t, groups)).wait_recv()
        for e in (1, 2, 0):
            edge(lb, e).start()
        for g in range(groups):
            at = (g * share + lb) * CELLS
            vox_ref[:, at : at + CELLS] = tab_ref[0, lb, g * width : (g + 1) * width]

    def pass_on(lb):
        edge(lb, 1).wait_recv()
        edge(lb, 5).start()
        edge(lb, 3).start()
        edge(lb, 2).wait_recv()
        edge(lb, 6).start()
        edge(lb, 4).start()

    def pass_last(lb):
        edge(lb, 5).wait_recv()
        edge(lb, 6).wait_recv()
        edge(lb, 7).start()

    spots = lax.broadcasted_iota(jnp.int32, (CELLS, rows), 0)

    def place(r):
        value = me
        for bit in (1, 2, 4):
            value = value + bit * (lax.rem(lax.rem(me // bit, 2) + lax.rem(r // bit, 2), 2) - lax.rem(me // bit, 2))
        return pl.ds(pl.multiple_of(value * rows, rows), rows)

    def pick(r, lb):
        ids = sid_ref[r]
        high = ids // CELLS
        low = ids % CELLS
        onehot = jnp.where(spots == low, 1.0, 0.0).astype(jnp.bfloat16)
        found = jnp.dot(tab_ref[r, lb], onehot, preferred_element_type=jnp.float32)
        at = place(r)
        total = jnp.zeros((width, rows), jnp.float32) if lb == 0 else pick_ref[:, at].astype(jnp.float32)
        for g in range(groups):
            total = jnp.where(
                jnp.broadcast_to(high, total.shape) == g * share + lb, found[g * width : (g + 1) * width], total
            )
        pick_ref[:, at] = total.astype(jnp.bfloat16)

    def picks(lo, hi, lb):
        def step(r, carry):
            pick(r, lb)
            return carry

        lax.fori_loop(lo, hi, step, 0)

    for lb in range(share):
        conv(lb)
    for r in range(1, owners):
        id_copy(r).wait_recv()
    last = share - 1
    gather_back(0)
    picks(0, 1, 0)
    for lb in range(1, share):
        gather_back(lb)
    edge(0, 0).wait_recv()
    picks(1, 2, 0)
    pass_on(0)
    edge(0, 3).wait_recv()
    edge(0, 4).wait_recv()
    picks(2, 6, 0)
    for lb in range(1, share):
        edge(lb, 0).wait_recv()
        picks(0, 2, lb)
        pass_on(lb)
        pass_last(lb - 1)
        edge(lb - 1, 7).wait_recv()
        picks(6, 8, lb - 1)
        edge(lb, 3).wait_recv()
        edge(lb, 4).wait_recv()
        picks(2, 6, lb)
    pass_last(last)
    picks(6, 7, last)
    edge(last, 7).wait_recv()
    picks(7, 8, last)
    for r in range(1, owners):
        id_copy(r).wait_send()
    for lb in range(share):
        for t in range(1, groups):
            back(lb, t, row).wait_send()
        for e in range(len(edges)):
            edge(lb, e).wait_send()


def finish(spread, weight_all, active, ids, share, owners, cap):
    halves, groups, _, part, outs = weight_all.shape
    width = halves * part
    wide = groups * width
    vmem = pl.BlockSpec(memory_space=pltpu.VMEM)
    dma = pltpu.SemaphoreType.DMA
    return pl.pallas_call(
        functools.partial(finish_kernel, share, owners),
        in_specs=[vmem] * 4,
        out_specs=[vmem, vmem],
        out_shape=[
            jax.ShapeDtypeStruct((width, groups * share * CELLS), jnp.bfloat16),
            jax.ShapeDtypeStruct((width, owners * cap), jnp.bfloat16),
        ],
        scratch_shapes=[
            pltpu.VMEM((share, ROWS, wide), jnp.float32),
            pltpu.VMEM((3, 6, 10, 16, wide), jnp.bfloat16),
            pltpu.VMEM((share, outs, CELLS), jnp.bfloat16),
            pltpu.VMEM((owners, share, wide, CELLS), jnp.bfloat16),
            pltpu.VMEM((owners, 1, cap), jnp.int32),
            dma((owners,)),
            dma((owners,)),
            dma((share, groups)),
            dma((share, groups)),
            dma((share, 8)),
            dma((share, 8)),
        ],
        compiler_params=remote_params(2),
    )(spread, weight_all, active, ids.reshape(owners, 1, cap))


def tally_cells(ids, cells):
    fine = 64
    high = (ids[None, :] // fine == jnp.arange(cells // fine, dtype=jnp.int32)[:, None]).astype(jnp.bfloat16)
    low = (ids[None, :] % fine == jnp.arange(fine, dtype=jnp.int32)[:, None]).astype(jnp.bfloat16)
    return lax.dot_general(high, low, (((1,), (1,)), ((), ())), preferred_element_type=jnp.float32).reshape(cells)


def gather_half(conv_weight):
    half = conv_weight.shape[1] // 2
    mine = lax.dynamic_slice_in_dim(conv_weight, lax.rem(lax.axis_index("space"), 2) * half, half, 1)
    return lax.all_gather(mine, "chan", axis=0)


def swap_halves(gathered, owners):
    pairs = [[i, i + 1] for i in range(0, owners, 2)]
    return lax.all_gather(gathered, "space", axis=0, axis_index_groups=pairs)


def on_device(points, point_cell, conv_weight, conv_bias, neighbors):
    width = points.shape[0]
    owners = lax.axis_size("space")
    groups = lax.axis_size("chan")
    cap = points.shape[2] // owners
    blocks = neighbors.shape[0]
    share = blocks // groups
    flat = points.reshape(width, owners * cap)
    ids = point_cell[0]
    gathered = gather_half(conv_weight)
    counts = tally_cells(ids, blocks * CELLS)
    active = jnp.where(counts > 0.0, 1.0, 0.0).astype(jnp.float32)
    own = pool(flat, ids, counts, groups, owners, cap)
    left = lax.ppermute(own, "space", [(i, i + 1) for i in range(owners - 1)])
    right = lax.ppermute(own, "space", [(i + 1, i) for i in range(owners - 1)])
    margins = build_margins(neighbors, left, own, right, conv_bias.reshape(1, width), groups, share)
    gathered, margins = lax.optimization_barrier((gathered, margins))
    weight_all = swap_halves(gathered, owners)
    spread = exchange(margins, "chan", 1)
    mine = lax.dynamic_slice_in_dim(active, lax.axis_index("chan") * (share * CELLS), share * CELLS, 0)
    mine = mine.reshape(1, share * CELLS)
    if owners == 8 and share > 1 and blocks * CELLS <= 2 * cap:
        voxel_out, picked = finish(spread, weight_all, mine, ids, share, owners, cap)
        point_out = (flat.astype(jnp.float32) + picked.astype(jnp.float32)).astype(jnp.bfloat16).reshape(points.shape)
        return (voxel_out, point_out)
    finished = convolve(spread, weight_all, mine, share)
    finished = finished.reshape(groups, width, share * CELLS)
    parts = exchange(finished, "chan", 2)
    voxel_out = jnp.transpose(parts, (1, 0, 2)).reshape(width, blocks * CELLS)
    point_out = give_back(parts, ids, flat, owners, cap).reshape(points.shape)
    return (voxel_out, point_out)


def solution(mesh):
    return jax.shard_map(
        on_device,
        mesh=mesh,
        in_specs=(
            P("chan", "space", None),
            P("space", None),
            P(None, "chan", None),
            P("chan"),
            P("space", None),
        ),
        out_specs=(P("chan", "space"), P("chan", "space", None)),
        check_vma=False,
    )
```

```python
import functools

import jax
import jax.numpy as jnp
from jax import lax
from jax.experimental import pallas as pl
from jax.experimental.pallas import tpu as pltpu
from jax.sharding import PartitionSpec as P

VMEM_LIMIT = 60 * 1024 * 1024
CELLS = 512
MESH = pl.DeviceIdType.MESH
ROWS = 1008


def params():
    return pltpu.CompilerParams(vmem_limit_bytes=VMEM_LIMIT)


def greet(axis, count):
    me = lax.axis_index(axis)
    barrier = pltpu.get_barrier_semaphore()

    def signal(t, carry):
        pl.semaphore_signal(barrier, inc=1, device_id={axis: lax.rem(me + t, count)}, device_id_type=MESH)
        return carry

    lax.fori_loop(1, count, signal, 0)
    pl.semaphore_wait(barrier, count - 1)
    return me


def remote_params(collective_id):
    return pltpu.CompilerParams(
        vmem_limit_bytes=VMEM_LIMIT, collective_id=collective_id, has_side_effects=True
    )


def pool_kernel(groups, low_cells, owners, x_ref, id_ref, count_ref, o_ref, held, acc_ref, send_sem, recv_sem, own_sem):
    width, rows = held.shape[1], held.shape[2]
    me = greet("space", owners)

    def chunk(d):
        return x_ref.at[:, pl.ds(pl.multiple_of(d * rows, rows), rows)]

    def copy(t):
        peer = lax.rem(me + t, owners)
        return pltpu.make_async_remote_copy(
            src_ref=chunk(peer),
            dst_ref=held.at[t],
            send_sem=send_sem.at[t],
            recv_sem=recv_sem.at[t],
            device_id={"space": peer},
            device_id_type=MESH,
        )

    def send(t, carry):
        copy(t).start()
        return carry

    lax.fori_loop(1, owners, send, 0)
    own = pltpu.make_async_copy(chunk(me), held.at[0], own_sem)
    own.start()
    acc_ref[...] = jnp.zeros_like(acc_ref)
    spots = lax.broadcasted_iota(jnp.int32, (low_cells, rows), 0)

    def add_chunk(t):
        ids = id_ref[lax.rem(me + owners - t, owners)]
        high = ids // low_cells
        low = ids % low_cells
        x = held[t]
        zero = jnp.zeros_like(x)
        masked = jnp.concatenate(
            [jnp.where(jnp.broadcast_to(high, x.shape) == g, x, zero) for g in range(groups)], axis=0
        )
        onehot = jnp.where(spots == low, 1.0, 0.0).astype(jnp.bfloat16)
        acc_ref[...] += lax.dot_general(
            onehot, masked, (((1,), (1,)), ((), ())), preferred_element_type=jnp.float32
        )

    own.wait()
    add_chunk(0)

    def take(t, carry):
        copy(t).wait_recv()
        add_chunk(t)
        return carry

    lax.fori_loop(1, owners, take, 0)
    for g in range(groups):
        lanes = slice(g * width, (g + 1) * width)
        tally = jnp.maximum(count_ref[:, g : g + 1], 1.0)
        o_ref[:, lanes] = (acc_ref[:, lanes] / tally).astype(jnp.bfloat16)

    def close(t, carry):
        copy(t).wait_send()
        return carry

    lax.fori_loop(1, owners, close, 0)


def pool(points, ids, counts, groups, owners, cap):
    width = points.shape[0]
    low_cells = counts.shape[0] // groups
    by_group = counts.reshape(groups, low_cells).T
    vmem = pl.BlockSpec(memory_space=pltpu.VMEM)
    return pl.pallas_call(
        functools.partial(pool_kernel, groups, low_cells, owners),
        in_specs=[pl.BlockSpec(memory_space=pl.ANY), vmem, vmem],
        out_specs=vmem,
        out_shape=jax.ShapeDtypeStruct((low_cells, groups * width), jnp.bfloat16),
        scratch_shapes=[
            pltpu.VMEM((owners, width, cap), jnp.bfloat16),
            pltpu.VMEM((low_cells, groups * width), jnp.float32),
            pltpu.SemaphoreType.DMA((owners,)),
            pltpu.SemaphoreType.DMA((owners,)),
            pltpu.SemaphoreType.DMA,
        ],
        compiler_params=remote_params(0),
    )(points, ids.reshape(owners, 1, cap), by_group)


def exchange_kernel(axis, count, x_ref, o_ref, send_sem, recv_sem):
    me = greet(axis, count)

    def copy(t, landing):
        peer = lax.rem(me + t, count)
        return pltpu.make_async_remote_copy(
            src_ref=x_ref.at[peer],
            dst_ref=o_ref.at[landing],
            send_sem=send_sem.at[t],
            recv_sem=recv_sem.at[t],
            device_id={axis: peer},
            device_id_type=MESH,
        )

    def send(t, carry):
        copy(t, me).start()
        return carry

    def close(t, carry):
        copy(t, lax.rem(me + count - t, count)).wait_recv()
        copy(t, me).wait_send()
        return carry

    lax.fori_loop(1, count, send, 0)
    o_ref[me] = x_ref[me]
    lax.fori_loop(1, count, close, 0)


def exchange(x, axis, collective_id):
    count = lax.axis_size(axis)
    vmem = pl.BlockSpec(memory_space=pltpu.VMEM)
    return pl.pallas_call(
        functools.partial(exchange_kernel, axis, count),
        in_specs=[vmem],
        out_specs=vmem,
        out_shape=jax.ShapeDtypeStruct(x.shape, x.dtype),
        scratch_shapes=[pltpu.SemaphoreType.DMA((count,)), pltpu.SemaphoreType.DMA((count,))],
        compiler_params=remote_params(collective_id),
    )(x)


def margin_kernel(groups, share, nb_ref, left_ref, own_ref, right_ref, bias_ref, o_ref, v_ref, m_ref):
    blocks = groups * share
    width = bias_ref.shape[1]
    for a, ref in enumerate((left_ref, own_ref, right_ref)):
        for g in range(groups):
            for lb in range(share):
                part = ref[lb * CELLS : (lb + 1) * CELLS, g * width : (g + 1) * width]
                v_ref[a * blocks + g * share + lb] = part.astype(jnp.float32).reshape(64, 8, width)
    v_ref[3 * blocks] = jnp.zeros((64, 8, width), jnp.float32)
    bias = jnp.broadcast_to(bias_ref[...].astype(jnp.float32), (8, width))
    spans = (((0, 7),), tuple((t + 1, t) for t in range(8)), ((9, 0),))

    def one_block(b, carry):
        for dx in range(3):
            for dy in range(3):
                for dz in range(3):
                    slot = nb_ref[b, 9 * dx + 3 * dy + dz]
                    slot = jnp.where(slot < 0, 3 * blocks, slot)
                    for xd, xs in spans[dx]:
                        for yd, ys in spans[dy]:
                            row = 100 * xd + 10 * yd
                            if dz == 1:
                                m_ref[b, row + 1 : row + 9, :] = v_ref[slot, 8 * xs + ys]
                            else:
                                zd, zs = spans[dz][0]
                                m_ref[b, row + zd : row + zd + 1, :] = v_ref[slot, 8 * xs + ys, zs : zs + 1, :]
        m_ref[b, 1000:ROWS, :] = bias
        return carry

    lax.fori_loop(0, blocks, one_block, 0)
    for g in range(groups):
        for lb in range(share):
            o_ref[g, :, lb * width : (lb + 1) * width] = m_ref[g * share + lb].astype(jnp.bfloat16)


def build_margins(neighbors, left, own, right, bias, groups, share):
    width = bias.shape[1]
    blocks = groups * share
    vmem = pl.BlockSpec(memory_space=pltpu.VMEM)
    return pl.pallas_call(
        functools.partial(margin_kernel, groups, share),
        in_specs=[pl.BlockSpec(memory_space=pltpu.SMEM), vmem, vmem, vmem, vmem],
        out_specs=vmem,
        out_shape=jax.ShapeDtypeStruct((groups, ROWS, share * width), jnp.bfloat16),
        scratch_shapes=[
            pltpu.VMEM((3 * blocks + 1, 64, 8, width), jnp.float32),
            pltpu.VMEM((blocks, ROWS, width), jnp.float32),
        ],
        compiler_params=params(),
    )(neighbors, left, own, right, bias)


def conv_kernel(share, m_ref, w_ref, act_ref, o_ref, f_ref, q_ref):
    halves, groups, _, part, outs = w_ref.shape
    width = halves * part
    wide = groups * width
    for lb in range(share):
        for g in range(groups):
            f_ref[lb, :, g * width : (g + 1) * width] = m_ref[g, :, lb * width : (lb + 1) * width].astype(jnp.float32)
    for k in range(3):
        for lb in range(share):
            for p in range(6):
                for y in range(10):
                    near = 100 * p + 10 * y + k
                    far = near + 400
                    q_ref[k, lb, p, y] = jnp.concatenate(
                        [f_ref[lb, near : near + 8, :], f_ref[lb, far : far + 8, :]], axis=0
                    ).astype(jnp.bfloat16)
    bias = f_ref[0, 1000:1001, :]
    for lb in range(share):
        total = None
        for k in range(3):
            windows, weights = [], []
            for i in range(3):
                for j in range(3):
                    windows.append(q_ref[k, lb, i : i + 4, j : j + 8].reshape(CELLS, wide))
                    for g in range(groups):
                        for half in range(halves):
                            weights.append(w_ref[half, g, 9 * i + 3 * j + k])
            term = jnp.dot(
                jnp.concatenate(windows, axis=1),
                jnp.concatenate(weights, axis=0),
                preferred_element_type=jnp.float32,
            )
            total = term if total is None else total + term
        total = jnp.maximum(total + bias, 0.0).reshape(4, 8, 2, 8, outs)
        for h in range(2):
            half = total[:, :, h].reshape(256, outs).T
            seg = slice(lb * CELLS + h * 256, lb * CELLS + (h + 1) * 256)
            o_ref[:, seg] = (half * act_ref[:, seg]).astype(jnp.bfloat16)


def convolve(spread, weight_all, active, share):
    halves, groups, _, part, outs = weight_all.shape
    vmem = pl.BlockSpec(memory_space=pltpu.VMEM)
    return pl.pallas_call(
        functools.partial(conv_kernel, share),
        in_specs=[vmem] * 3,
        out_specs=vmem,
        out_shape=jax.ShapeDtypeStruct((outs, share * CELLS), jnp.bfloat16),
        scratch_shapes=[
            pltpu.VMEM((share, ROWS, groups * halves * part), jnp.float32),
            pltpu.VMEM((3, share, 6, 10, 16, groups * halves * part), jnp.bfloat16),
        ],
        compiler_params=params(),
    )(spread, weight_all, active)


def return_kernel(groups, owners, v_ref, id_ref, p_ref, o_ref, found_ref, held, send_sem, recv_sem):
    width, low_cells = v_ref.shape[0] // groups, v_ref.shape[1]
    rows = id_ref.shape[2]
    me = greet("space", owners)
    spots = lax.broadcasted_iota(jnp.int32, (low_cells, rows), 0)

    def copy(t):
        return pltpu.make_async_remote_copy(
            src_ref=found_ref.at[t],
            dst_ref=held.at[t],
            send_sem=send_sem.at[t],
            recv_sem=recv_sem.at[t],
            device_id={"space": lax.rem(me + t, owners)},
            device_id_type=MESH,
        )

    def pick(s):
        ids = id_ref[s]
        high = ids // low_cells
        low = ids % low_cells
        onehot = jnp.where(spots == low, 1.0, 0.0).astype(jnp.bfloat16)
        found = jnp.dot(v_ref[...], onehot, preferred_element_type=jnp.float32)
        total = jnp.zeros((width, rows), jnp.float32)
        for g in range(groups):
            total = jnp.where(jnp.broadcast_to(high, total.shape) == g, found[g * width : (g + 1) * width], total)
        return total

    def add(d, values):
        at = pl.ds(pl.multiple_of(d * rows, rows), rows)
        o_ref[:, at] = (p_ref[:, at].astype(jnp.float32) + values).astype(jnp.bfloat16)

    def send(t, carry):
        found_ref[t] = pick(lax.rem(me + t, owners)).astype(jnp.bfloat16)
        copy(t).start()
        return carry

    def take(t, carry):
        copy(t).wait_recv()
        add(lax.rem(me + owners - t, owners), held[t].astype(jnp.float32))
        return carry

    def close(t, carry):
        copy(t).wait_send()
        return carry

    lax.fori_loop(1, owners, send, 0)
    add(me, pick(me))
    lax.fori_loop(1, owners, take, 0)
    lax.fori_loop(1, owners, close, 0)


def give_back(parts, ids, points, owners, cap):
    groups, width, low_cells = parts.shape
    vmem = pl.BlockSpec(memory_space=pltpu.VMEM)
    return pl.pallas_call(
        functools.partial(return_kernel, groups, owners),
        in_specs=[vmem] * 3,
        out_specs=vmem,
        out_shape=jax.ShapeDtypeStruct(points.shape, jnp.bfloat16),
        scratch_shapes=[
            pltpu.VMEM((owners, width, cap), jnp.bfloat16),
            pltpu.VMEM((owners, width, cap), jnp.bfloat16),
            pltpu.SemaphoreType.DMA((owners,)),
            pltpu.SemaphoreType.DMA((owners,)),
        ],
        compiler_params=remote_params(3),
    )(parts.reshape(groups * width, low_cells), ids.reshape(owners, 1, cap), points)


SIDE = tuple((x, y) for x in range(10) for y in range(10) if x in (0, 9) or y in (0, 9))
LOW_AT, HIGH_AT = 288, 392
EDGES = (
    (0, 1, 1, 0),
    (0, 2, 2, 0),
    (0, 4, 4, 0),
    (2, 3, 1, 0),
    (4, 5, 1, 0),
    (2, 6, 4, 1),
    (4, 6, 2, 2),
    (6, 7, 1, 0),
)


def partner(me, mask):
    value = me
    for bit in (1, 2, 4):
        mine = lax.rem(me // bit, 2)
        value = value + bit * (lax.rem(mine + lax.rem(mask // bit, 2), 2) - mine)
    return value


def toward(padded):
    if padded == 0:
        return 0, 7
    if padded == 9:
        return 2, 0
    return 1, padded - 1


def whole_kernel(
    share, owners, pieces, nb_ref, x_ref, id_ref, bias_ref, w_ref, vox_ref, pick_ref,
    held, acc_ref, cnt_ref, own_ref, near_ref, v_ref, zp_ref, sh_ref, shout_ref, cen_ref, shin_ref,
    f_ref, q_ref, sum_ref, wall_ref, bown_ref, ball_ref, fin_ref, tab_ref, sid_ref,
    pool_send, pool_recv, cen_send, cen_recv, shell_send, shell_recv, halo_send, halo_recv,
    w_send, w_recv, wsib_send, wsib_recv, bias_send, bias_recv,
    id_send, id_recv, back_send, back_recv, tab_send, tab_recv, own_sem, wown_sem,
):
    _, width, outs = w_ref.shape
    groups = outs // width
    cw = width // pieces
    blocks = groups * share
    rows = id_ref.shape[2]
    split = outs // 2
    me = lax.axis_index("space")
    row = lax.axis_index("chan")
    parity = lax.rem(me, 2)
    barrier = pltpu.get_barrier_semaphore()
    for r in range(1, owners):
        pl.semaphore_signal(barrier, inc=1, device_id={"space": partner(me, r)}, device_id_type=MESH)
    for t in range(1, groups):
        pl.semaphore_signal(barrier, inc=1, device_id={"chan": lax.rem(row + t, groups)}, device_id_type=MESH)
    pl.semaphore_wait(barrier, owners + groups - 2)

    def remote(src, dst, send, recv, device):
        return pltpu.make_async_remote_copy(
            src_ref=src, dst_ref=dst, send_sem=send, recv_sem=recv, device_id=device, device_id_type=MESH
        )

    def ahead(t):
        return lax.rem(row + t, groups)

    def behind(t):
        return lax.rem(row + groups - t, groups)

    def channels(h):
        return slice(h * cw, (h + 1) * cw)

    def slots(d):
        return pl.ds(pl.multiple_of(d * rows, rows), rows)

    def pool_copy(h, r):
        peer = partner(me, r)
        return remote(
            x_ref.at[channels(h), slots(peer)], held.at[r, channels(h)],
            pool_send.at[h, r], pool_recv.at[h, r], {"space": peer},
        )

    def id_copy(r):
        peer = partner(me, r)
        return remote(id_ref.at[peer], sid_ref.at[r], id_send.at[r], id_recv.at[r], {"space": peer})

    def bias_copy(t, landing):
        return remote(bown_ref, ball_ref.at[landing], bias_send.at[t], bias_recv.at[t], {"chan": ahead(t)})

    def w_copy(t, landing):
        half = pl.ds(pl.multiple_of(parity * cw, cw), cw)
        return remote(
            w_ref.at[:, half], wall_ref.at[parity, landing], w_send.at[t], w_recv.at[t], {"chan": ahead(t)}
        )

    def w_swap(t, half):
        return remote(
            wall_ref.at[parity, behind(t)], wall_ref.at[half, behind(t)],
            wsib_send.at[t], wsib_recv.at[t], {"space": partner(me, 1)},
        )

    def cen_copy(h, t, landing):
        return remote(
            own_ref.at[h, ahead(t)], cen_ref.at[h, landing],
            cen_send.at[h, t], cen_recv.at[h, t], {"chan": ahead(t)},
        )

    def shell_copy(h, t, landing):
        return remote(
            shout_ref.at[h, ahead(t)], shin_ref.at[h, landing],
            shell_send.at[h, t], shell_recv.at[h, t], {"chan": ahead(t)},
        )

    def to_right(h):
        return remote(
            own_ref.at[h], near_ref.at[h, 0], halo_send.at[h, 0], halo_recv.at[h, 0],
            {"space": lax.rem(me + 1, owners)},
        )

    def to_left(h):
        return remote(
            own_ref.at[h], near_ref.at[h, 1], halo_send.at[h, 1], halo_recv.at[h, 1],
            {"space": lax.rem(me + owners - 1, owners)},
        )

    def lane_rows(index):
        return pl.ds(pl.multiple_of(index * width, width), width)

    def back(lb, t, landing):
        return remote(
            fin_ref.at[lb, lane_rows(ahead(t))], tab_ref.at[0, lb, lane_rows(landing)],
            back_send.at[lb, t], back_recv.at[lb, t], {"chan": ahead(t)},
        )

    def edge(lb, e):
        source, target, mask, part = EDGES[e]
        span = (slice(0, outs), slice(0, split), slice(split, outs))[part]
        return remote(
            tab_ref.at[source, lb, span], tab_ref.at[target, lb, span],
            tab_send.at[lb, e], tab_recv.at[lb, e], {"space": partner(me, mask)},
        )

    def send_pool(r, carry):
        pool_copy(0, r).start()
        return carry

    lax.fori_loop(1, owners, send_pool, 0)
    for t in range(1, groups):
        w_copy(t, row).start()
    own = pltpu.make_async_copy(x_ref.at[:, slots(me)], held.at[0], own_sem)
    own.start()
    own_w = [
        pltpu.make_async_copy(w_ref.at[:, channels(h)], wall_ref.at[h, row], wown_sem.at[h]) for h in range(pieces)
    ]
    for copy in own_w:
        copy.start()
    bown_ref[:, 0:width] = jnp.broadcast_to(bias_ref[...].astype(jnp.float32), (8, width))
    for t in range(1, groups):
        bias_copy(t, row).start()
    ball_ref[row] = bown_ref[...]
    for r in range(1, owners):
        id_copy(r).start()
    sid_ref[0] = id_ref[me]
    v_ref[3 * blocks] = jnp.zeros(v_ref.shape[1:], jnp.float32)
    for h in range(pieces):
        @pl.when(me == 0)
        def _():
            near_ref[h, 0] = jnp.zeros(near_ref.shape[2:], jnp.bfloat16)

        @pl.when(me == owners - 1)
        def _():
            near_ref[h, 1] = jnp.zeros(near_ref.shape[2:], jnp.bfloat16)

    spots = lax.broadcasted_iota(jnp.int32, (CELLS, rows), 0)

    def locate(ids):
        onehot = jnp.where(spots == ids % CELLS, 1.0, 0.0).astype(jnp.bfloat16)
        return ids // CELLS, onehot

    def add_chunk(h, r):
        high, onehot = locate(id_ref[partner(me, r)])
        x = held[r, channels(h)]
        wide_high = jnp.broadcast_to(high, x.shape)
        zero = jnp.zeros_like(x)
        nt = (((1,), (1,)), ((), ()))
        masked = jnp.concatenate([jnp.where(wide_high == g, x, zero) for g in range(blocks)], axis=0)
        acc_ref[...] += lax.dot_general(onehot, masked, nt, preferred_element_type=jnp.float32)
        if h == 0:
            one = jnp.ones_like(x)
            hot = jnp.concatenate([jnp.where(wide_high == g, one, zero) for g in range(blocks)], axis=0)
            cnt_ref[...] += lax.dot_general(onehot, hot, nt, preferred_element_type=jnp.float32)

    def take(h, lo, hi):
        def step(r, carry):
            pool_copy(h, r).wait_recv()
            if h + 1 < pieces:
                pool_copy(h + 1, r).start()
            add_chunk(h, r)
            return carry

        lax.fori_loop(lo, hi, step, 0)

    def normalise(h):
        v = (acc_ref[...] / jnp.maximum(cnt_ref[...], 1.0)).astype(jnp.bfloat16)
        lanes = share * cw
        for j in range(groups):
            at = slice(j * lanes, (j + 1) * lanes)
            own_ref[h, j] = jnp.concatenate([v[:256, at], v[256:, at]], axis=1)

        @pl.when(me < owners - 1)
        def _():
            to_right(h).start()

        @pl.when(me > 0)
        def _():
            to_left(h).start()

        for t in range(1, groups):
            cen_copy(h, t, row).start()
        cen_ref[h, row] = own_ref[h, row]

    def load_slots(a, part):
        for j in range(groups):
            for half in range(2):
                for lb in range(share):
                    at = (half * share + lb) * cw
                    slot = a * blocks + j * share + lb
                    v_ref[slot, half * 256 : (half + 1) * 256, 0:cw] = part[j, :, at : at + cw].astype(jnp.float32)
        for b in range(blocks):
            slot = a * blocks + b
            zp_ref[slot, 0] = v_ref[slot, pl.ds(7, 64, stride=8), :]
            zp_ref[slot, 1] = v_ref[slot, pl.ds(0, 64, stride=8), :]

    def shell(h):
        @pl.when(me > 0)
        def _():
            to_right(h).wait_recv()

        @pl.when(me < owners - 1)
        def _():
            to_left(h).wait_recv()

        load_slots(0, near_ref.at[h, 0])
        load_slots(2, near_ref.at[h, 1])

        def one_block(b, carry):
            def slot_of(o):
                slot = nb_ref[b, o]
                return jnp.where(slot < 0, 3 * blocks, slot)

            for c, (xd, yd) in enumerate(SIDE):
                (dx, xs), (dy, ys) = toward(xd), toward(yd)
                at = 8 * (8 * xs + ys)
                sh_ref[b, 8 * c : 8 * c + 8, :] = v_ref[slot_of(9 * dx + 3 * dy + 1), at : at + 8, :]
            for z, (base, dz) in enumerate(((LOW_AT, 0), (HIGH_AT, 2))):
                for xd in range(10):
                    dx, xs = toward(xd)
                    to = base + 10 * xd
                    at = 8 * xs
                    o = 9 * dx + dz
                    sh_ref[b, to + 1 : to + 9, :] = zp_ref[slot_of(o + 3), z, at : at + 8, :]
                    sh_ref[b, to : to + 1, :] = zp_ref[slot_of(o), z, at + 7 : at + 8, :]
                    sh_ref[b, to + 9 : to + 10, :] = zp_ref[slot_of(o + 6), z, at : at + 1, :]
            return carry

        lax.fori_loop(0, blocks, one_block, 0)
        for j in range(groups):
            shout_ref[h, j] = jnp.concatenate(
                [
                    sh_ref[j * share + lb, half * 256 : (half + 1) * 256, 0:cw]
                    for half in range(2)
                    for lb in range(share)
                ],
                axis=1,
            ).astype(jnp.bfloat16)
        for t in range(1, groups):
            shell_copy(h, t, row).start()
        shin_ref[h, row] = shout_ref[h, row]

    def joined(ref, h, lb, half):
        at = (half * share + lb) * cw
        return jnp.concatenate([ref[h, g, :, at : at + cw] for g in range(groups)], axis=1).astype(jnp.float32)

    def unpack_center(h):
        for t in range(1, groups):
            cen_copy(h, t, behind(t)).wait_recv()
        for lb in range(share):
            for half in range(2):
                part = joined(cen_ref, h, lb, half)
                for x in range(4):
                    for y in range(8):
                        to = 100 * (4 * half + x + 1) + 10 * (y + 1) + 1
                        at = 8 * (8 * x + y)
                        f_ref[lb, to : to + 8, :] = part[at : at + 8]

    def unpack_shell(h):
        for t in range(1, groups):
            shell_copy(h, t, behind(t)).wait_recv()
        for lb in range(share):
            first, second = joined(shin_ref, h, lb, 0), joined(shin_ref, h, lb, 1)
            for c, (xd, yd) in enumerate(SIDE):
                to = 100 * xd + 10 * yd + 1
                at = 8 * c
                f_ref[lb, to : to + 8, :] = first[at : at + 8] if at < 256 else second[at - 256 : at - 248]
            f_ref[lb, pl.ds(0, 100, stride=10), :] = second[LOW_AT - 256 : LOW_AT - 156]
            f_ref[lb, pl.ds(9, 100, stride=10), :] = second[HIGH_AT - 256 : HIGH_AT - 156]

    def windows_of(lb):
        for k in range(3):
            for p in range(6):
                for y in range(10):
                    near = 100 * p + 10 * y + k
                    far = near + 400
                    q_ref[lb, k, p, y] = jnp.concatenate(
                        [f_ref[lb, near : near + 8, :], f_ref[lb, far : far + 8, :]], axis=0
                    ).astype(jnp.bfloat16)

    def conv(h, lb):
        windows, weights = [], []
        for k in range(3):
            for i in range(3):
                for j in range(3):
                    windows.append(q_ref[lb, k, i : i + 4, j : j + 8].reshape(CELLS, groups * cw))
                    for g in range(groups):
                        weights.append(wall_ref[h, g, 9 * i + 3 * j + k])
        return jnp.dot(
            jnp.concatenate(windows, axis=1), jnp.concatenate(weights, axis=0), preferred_element_type=jnp.float32
        )

    def close_conv(lb, total):
        bias = jnp.concatenate([ball_ref[g, 0:1, 0:width] for g in range(groups)], axis=1)
        lane = lax.broadcasted_iota(jnp.int32, cnt_ref.shape, 1)
        mine = jnp.where(lane == (row * share + lb) * cw, cnt_ref[...], 0.0)
        active = jnp.where(jnp.sum(mine, axis=1, keepdims=True) > 0.0, 1.0, 0.0)
        total = jnp.maximum(total + bias, 0.0).reshape(4, 8, 2, 8, outs)
        for half in range(2):
            seg = slice(half * 256, (half + 1) * 256)
            fin_ref[lb, :, seg] = (total[:, :, half].reshape(256, outs) * active[seg]).T.astype(jnp.bfloat16)
        for t in range(1, groups):
            back(lb, t, row).start()
        tab_ref[0, lb, lane_rows(row)] = fin_ref[lb, lane_rows(row)]

    def gather_back(lb):
        for t in range(1, groups):
            back(lb, t, behind(t)).wait_recv()
        for e in (1, 2, 0):
            edge(lb, e).start()
        for g in range(groups):
            at = (g * share + lb) * CELLS
            vox_ref[:, at : at + CELLS] = tab_ref[0, lb, g * width : (g + 1) * width]

    def pass_on(lb):
        edge(lb, 1).wait_recv()
        edge(lb, 5).start()
        edge(lb, 3).start()
        edge(lb, 2).wait_recv()
        edge(lb, 6).start()
        edge(lb, 4).start()

    def pass_last(lb):
        edge(lb, 5).wait_recv()
        edge(lb, 6).wait_recv()
        edge(lb, 7).start()

    def pick(r, lb):
        high, onehot = locate(sid_ref[r])
        found = jnp.dot(tab_ref[r, lb], onehot, preferred_element_type=jnp.float32)
        at = slots(partner(me, r))
        total = jnp.zeros((width, rows), jnp.float32) if lb == 0 else pick_ref[:, at].astype(jnp.float32)
        for g in range(groups):
            total = jnp.where(
                jnp.broadcast_to(high, total.shape) == g * share + lb, found[g * width : (g + 1) * width], total
            )
        pick_ref[:, at] = total.astype(jnp.bfloat16)

    def picks(lo, hi, lb):
        def step(r, carry):
            pick(r, lb)
            return carry

        lax.fori_loop(lo, hi, step, 0)

    acc_ref[...] = jnp.zeros_like(acc_ref)
    cnt_ref[...] = jnp.zeros_like(cnt_ref)
    own.wait()
    add_chunk(0, 0)
    take(0, 1, owners)
    normalise(0)
    load_slots(1, own_ref.at[0])
    acc_ref[...] = jnp.zeros_like(acc_ref)
    add_chunk(1, 0)
    take(1, 1, 4)
    shell(0)
    take(1, 4, owners)
    normalise(1)
    load_slots(1, own_ref.at[1])
    for t in range(1, groups):
        w_copy(t, behind(t)).wait_recv()
        w_swap(t, parity).start()
    unpack_center(0)
    unpack_shell(0)
    for lb in range(share):
        windows_of(lb)
    shell(1)
    for copy in own_w:
        copy.wait()
    for t in range(1, groups):
        w_swap(t, 1 - parity).wait_recv()
        bias_copy(t, behind(t)).wait_recv()
    for r in range(1, owners):
        id_copy(r).wait_recv()
    for lb in range(share):
        sum_ref[lb] = conv(0, lb)
    unpack_center(1)
    unpack_shell(1)
    for lb in range(share):
        windows_of(lb)
        close_conv(lb, sum_ref[lb] + conv(1, lb))
    gather_back(0)
    picks(0, 1, 0)
    gather_back(1)
    edge(0, 0).wait_recv()
    picks(1, 2, 0)
    pass_on(0)
    edge(0, 3).wait_recv()
    edge(0, 4).wait_recv()
    picks(2, 6, 0)
    edge(1, 0).wait_recv()
    picks(0, 2, 1)
    pass_on(1)
    pass_last(0)
    edge(0, 7).wait_recv()
    picks(6, 8, 0)
    edge(1, 3).wait_recv()
    edge(1, 4).wait_recv()
    picks(2, 6, 1)
    pass_last(1)
    picks(6, 7, 1)
    edge(1, 7).wait_recv()
    picks(7, 8, 1)

    for h in range(pieces):
        def close(r, carry):
            pool_copy(h, r).wait_send()
            return carry

        lax.fori_loop(1, owners, close, 0)

        @pl.when(me < owners - 1)
        def _():
            to_right(h).wait_send()

        @pl.when(me > 0)
        def _():
            to_left(h).wait_send()

        for t in range(1, groups):
            cen_copy(h, t, row).wait_send()
            shell_copy(h, t, row).wait_send()
    for t in range(1, groups):
        w_copy(t, row).wait_send()
        w_swap(t, parity).wait_send()
        bias_copy(t, row).wait_send()
    for r in range(1, owners):
        id_copy(r).wait_send()
    for lb in range(share):
        for t in range(1, groups):
            back(lb, t, row).wait_send()
        for e in range(len(EDGES)):
            edge(lb, e).wait_send()


def whole(neighbors, points, ids, bias, weight, groups, share, owners, cap):
    pieces = 2
    _, width, outs = weight.shape
    cw = width // pieces
    blocks = groups * share
    lanes = 2 * share * cw
    vmem = pl.BlockSpec(memory_space=pltpu.VMEM)
    anywhere = pl.BlockSpec(memory_space=pl.ANY)
    dma = pltpu.SemaphoreType.DMA
    bf16, f32 = jnp.bfloat16, jnp.float32
    return pl.pallas_call(
        functools.partial(whole_kernel, share, owners, pieces),
        in_specs=[pl.BlockSpec(memory_space=pltpu.SMEM), anywhere, vmem, vmem, anywhere],
        out_specs=[vmem, vmem],
        out_shape=[
            jax.ShapeDtypeStruct((width, blocks * CELLS), bf16),
            jax.ShapeDtypeStruct((width, owners * cap), bf16),
        ],
        scratch_shapes=[
            pltpu.VMEM((owners, width, cap), bf16),
            pltpu.VMEM((CELLS, blocks * cw), f32),
            pltpu.VMEM((CELLS, blocks * cw), f32),
            pltpu.VMEM((pieces, groups, 256, lanes), bf16),
            pltpu.VMEM((pieces, 2, groups, 256, lanes), bf16),
            pltpu.VMEM((3 * blocks + 1, CELLS, 128), f32),
            pltpu.VMEM((3 * blocks + 1, 2, 64, 128), f32),
            pltpu.VMEM((blocks, CELLS, 128), f32),
            pltpu.VMEM((pieces, groups, 256, lanes), bf16),
            pltpu.VMEM((pieces, groups, 256, lanes), bf16),
            pltpu.VMEM((pieces, groups, 256, lanes), bf16),
            pltpu.VMEM((share, ROWS, groups * cw), f32),
            pltpu.VMEM((share, 3, 6, 10, 16, groups * cw), bf16),
            pltpu.VMEM((share, CELLS, outs), f32),
            pltpu.VMEM((pieces, groups, 27, cw, outs), bf16),
            pltpu.VMEM((8, 128), f32),
            pltpu.VMEM((groups, 8, 128), f32),
            pltpu.VMEM((share, outs, CELLS), bf16),
            pltpu.VMEM((owners, share, outs, CELLS), bf16),
            pltpu.VMEM((owners, 1, cap), jnp.int32),
            dma((pieces, owners)),
            dma((pieces, owners)),
            dma((pieces, groups)),
            dma((pieces, groups)),
            dma((pieces, groups)),
            dma((pieces, groups)),
            dma((pieces, 2)),
            dma((pieces, 2)),
            dma((groups,)),
            dma((groups,)),
            dma((groups,)),
            dma((groups,)),
            dma((groups,)),
            dma((groups,)),
            dma((owners,)),
            dma((owners,)),
            dma((share, groups)),
            dma((share, groups)),
            dma((share, len(EDGES))),
            dma((share, len(EDGES))),
            dma,
            dma((pieces,)),
        ],
        compiler_params=remote_params(4),
    )(neighbors, points, ids.reshape(owners, 1, cap), bias, weight)


def tally_cells(ids, cells):
    fine = 64
    high = (ids[None, :] // fine == jnp.arange(cells // fine, dtype=jnp.int32)[:, None]).astype(jnp.bfloat16)
    low = (ids[None, :] % fine == jnp.arange(fine, dtype=jnp.int32)[:, None]).astype(jnp.bfloat16)
    return lax.dot_general(high, low, (((1,), (1,)), ((), ())), preferred_element_type=jnp.float32).reshape(cells)


def gather_half(conv_weight):
    half = conv_weight.shape[1] // 2
    mine = lax.dynamic_slice_in_dim(conv_weight, lax.rem(lax.axis_index("space"), 2) * half, half, 1)
    return lax.all_gather(mine, "chan", axis=0)


def swap_halves(gathered, owners):
    pairs = [[i, i + 1] for i in range(0, owners, 2)]
    return lax.all_gather(gathered, "space", axis=0, axis_index_groups=pairs)


def on_device(points, point_cell, conv_weight, conv_bias, neighbors):
    width = points.shape[0]
    owners = lax.axis_size("space")
    groups = lax.axis_size("chan")
    cap = points.shape[2] // owners
    blocks = neighbors.shape[0]
    share = blocks // groups
    flat = points.reshape(width, owners * cap)
    ids = point_cell[0]
    if owners == 8 and share == 2 and width == 64 and groups == 4:
        voxel_out, picked = whole(
            neighbors, flat, ids, conv_bias.reshape(1, width), conv_weight, groups, share, owners, cap
        )
        point_out = flat.astype(jnp.float32) + picked.astype(jnp.float32)
        return (voxel_out, point_out.astype(jnp.bfloat16).reshape(points.shape))
    gathered = gather_half(conv_weight)
    counts = tally_cells(ids, blocks * CELLS)
    active = jnp.where(counts > 0.0, 1.0, 0.0).astype(jnp.float32)
    own = pool(flat, ids, counts, groups, owners, cap)
    left = lax.ppermute(own, "space", [(i, i + 1) for i in range(owners - 1)])
    right = lax.ppermute(own, "space", [(i + 1, i) for i in range(owners - 1)])
    margins = build_margins(neighbors, left, own, right, conv_bias.reshape(1, width), groups, share)
    gathered, margins = lax.optimization_barrier((gathered, margins))
    weight_all = swap_halves(gathered, owners)
    spread = exchange(margins, "chan", 1)
    mine = lax.dynamic_slice_in_dim(active, lax.axis_index("chan") * (share * CELLS), share * CELLS, 0)
    finished = convolve(spread, weight_all, mine.reshape(1, share * CELLS), share)
    finished = finished.reshape(groups, width, share * CELLS)
    parts = exchange(finished, "chan", 2)
    voxel_out = jnp.transpose(parts, (1, 0, 2)).reshape(width, blocks * CELLS)
    point_out = give_back(parts, ids, flat, owners, cap).reshape(points.shape)
    return (voxel_out, point_out)


def solution(mesh):
    return jax.shard_map(
        on_device,
        mesh=mesh,
        in_specs=(
            P("chan", "space", None),
            P("space", None),
            P(None, "chan", None),
            P("chan"),
            P("space", None),
        ),
        out_specs=(P("chan", "space"), P("chan", "space", None)),
        check_vma=False,
    )
```

```python
import functools

import jax
import jax.numpy as jnp
from jax import lax
from jax.experimental import pallas as pl
from jax.experimental.pallas import tpu as pltpu
from jax.sharding import PartitionSpec as P

VMEM_LIMIT = 60 * 1024 * 1024
CELLS = 512
MESH = pl.DeviceIdType.MESH
ROWS = 1008


def params():
    return pltpu.CompilerParams(vmem_limit_bytes=VMEM_LIMIT)


def greet(axis, count):
    me = lax.axis_index(axis)
    barrier = pltpu.get_barrier_semaphore()

    def signal(t, carry):
        pl.semaphore_signal(barrier, inc=1, device_id={axis: lax.rem(me + t, count)}, device_id_type=MESH)
        return carry

    lax.fori_loop(1, count, signal, 0)
    pl.semaphore_wait(barrier, count - 1)
    return me


def remote_params(collective_id):
    return pltpu.CompilerParams(
        vmem_limit_bytes=VMEM_LIMIT, collective_id=collective_id, has_side_effects=True
    )


def pool_kernel(groups, low_cells, owners, x_ref, id_ref, count_ref, o_ref, held, acc_ref, send_sem, recv_sem, own_sem):
    width, rows = held.shape[1], held.shape[2]
    me = greet("space", owners)

    def chunk(d):
        return x_ref.at[:, pl.ds(pl.multiple_of(d * rows, rows), rows)]

    def copy(t):
        peer = lax.rem(me + t, owners)
        return pltpu.make_async_remote_copy(
            src_ref=chunk(peer),
            dst_ref=held.at[t],
            send_sem=send_sem.at[t],
            recv_sem=recv_sem.at[t],
            device_id={"space": peer},
            device_id_type=MESH,
        )

    def send(t, carry):
        copy(t).start()
        return carry

    lax.fori_loop(1, owners, send, 0)
    own = pltpu.make_async_copy(chunk(me), held.at[0], own_sem)
    own.start()
    acc_ref[...] = jnp.zeros_like(acc_ref)
    spots = lax.broadcasted_iota(jnp.int32, (low_cells, rows), 0)

    def add_chunk(t):
        ids = id_ref[lax.rem(me + owners - t, owners)]
        high = ids // low_cells
        low = ids % low_cells
        x = held[t]
        zero = jnp.zeros_like(x)
        masked = jnp.concatenate(
            [jnp.where(jnp.broadcast_to(high, x.shape) == g, x, zero) for g in range(groups)], axis=0
        )
        onehot = jnp.where(spots == low, 1.0, 0.0).astype(jnp.bfloat16)
        acc_ref[...] += lax.dot_general(
            onehot, masked, (((1,), (1,)), ((), ())), preferred_element_type=jnp.float32
        )

    own.wait()
    add_chunk(0)

    def take(t, carry):
        copy(t).wait_recv()
        add_chunk(t)
        return carry

    lax.fori_loop(1, owners, take, 0)
    for g in range(groups):
        lanes = slice(g * width, (g + 1) * width)
        tally = jnp.maximum(count_ref[:, g : g + 1], 1.0)
        o_ref[:, lanes] = (acc_ref[:, lanes] / tally).astype(jnp.bfloat16)

    def close(t, carry):
        copy(t).wait_send()
        return carry

    lax.fori_loop(1, owners, close, 0)


def pool(points, ids, counts, groups, owners, cap):
    width = points.shape[0]
    low_cells = counts.shape[0] // groups
    by_group = counts.reshape(groups, low_cells).T
    vmem = pl.BlockSpec(memory_space=pltpu.VMEM)
    return pl.pallas_call(
        functools.partial(pool_kernel, groups, low_cells, owners),
        in_specs=[pl.BlockSpec(memory_space=pl.ANY), vmem, vmem],
        out_specs=vmem,
        out_shape=jax.ShapeDtypeStruct((low_cells, groups * width), jnp.bfloat16),
        scratch_shapes=[
            pltpu.VMEM((owners, width, cap), jnp.bfloat16),
            pltpu.VMEM((low_cells, groups * width), jnp.float32),
            pltpu.SemaphoreType.DMA((owners,)),
            pltpu.SemaphoreType.DMA((owners,)),
            pltpu.SemaphoreType.DMA,
        ],
        compiler_params=remote_params(0),
    )(points, ids.reshape(owners, 1, cap), by_group)


def exchange_kernel(axis, count, x_ref, o_ref, send_sem, recv_sem):
    me = greet(axis, count)

    def copy(t, landing):
        peer = lax.rem(me + t, count)
        return pltpu.make_async_remote_copy(
            src_ref=x_ref.at[peer],
            dst_ref=o_ref.at[landing],
            send_sem=send_sem.at[t],
            recv_sem=recv_sem.at[t],
            device_id={axis: peer},
            device_id_type=MESH,
        )

    def send(t, carry):
        copy(t, me).start()
        return carry

    def close(t, carry):
        copy(t, lax.rem(me + count - t, count)).wait_recv()
        copy(t, me).wait_send()
        return carry

    lax.fori_loop(1, count, send, 0)
    o_ref[me] = x_ref[me]
    lax.fori_loop(1, count, close, 0)


def exchange(x, axis, collective_id):
    count = lax.axis_size(axis)
    vmem = pl.BlockSpec(memory_space=pltpu.VMEM)
    return pl.pallas_call(
        functools.partial(exchange_kernel, axis, count),
        in_specs=[vmem],
        out_specs=vmem,
        out_shape=jax.ShapeDtypeStruct(x.shape, x.dtype),
        scratch_shapes=[pltpu.SemaphoreType.DMA((count,)), pltpu.SemaphoreType.DMA((count,))],
        compiler_params=remote_params(collective_id),
    )(x)


def margin_kernel(groups, share, nb_ref, left_ref, own_ref, right_ref, bias_ref, o_ref, v_ref, m_ref):
    blocks = groups * share
    width = bias_ref.shape[1]
    for a, ref in enumerate((left_ref, own_ref, right_ref)):
        for g in range(groups):
            for lb in range(share):
                part = ref[lb * CELLS : (lb + 1) * CELLS, g * width : (g + 1) * width]
                v_ref[a * blocks + g * share + lb] = part.astype(jnp.float32).reshape(64, 8, width)
    v_ref[3 * blocks] = jnp.zeros((64, 8, width), jnp.float32)
    bias = jnp.broadcast_to(bias_ref[...].astype(jnp.float32), (8, width))
    spans = (((0, 7),), tuple((t + 1, t) for t in range(8)), ((9, 0),))

    def one_block(b, carry):
        for dx in range(3):
            for dy in range(3):
                for dz in range(3):
                    slot = nb_ref[b, 9 * dx + 3 * dy + dz]
                    slot = jnp.where(slot < 0, 3 * blocks, slot)
                    for xd, xs in spans[dx]:
                        for yd, ys in spans[dy]:
                            row = 100 * xd + 10 * yd
                            if dz == 1:
                                m_ref[b, row + 1 : row + 9, :] = v_ref[slot, 8 * xs + ys]
                            else:
                                zd, zs = spans[dz][0]
                                m_ref[b, row + zd : row + zd + 1, :] = v_ref[slot, 8 * xs + ys, zs : zs + 1, :]
        m_ref[b, 1000:ROWS, :] = bias
        return carry

    lax.fori_loop(0, blocks, one_block, 0)
    for g in range(groups):
        for lb in range(share):
            o_ref[g, :, lb * width : (lb + 1) * width] = m_ref[g * share + lb].astype(jnp.bfloat16)


def build_margins(neighbors, left, own, right, bias, groups, share):
    width = bias.shape[1]
    blocks = groups * share
    vmem = pl.BlockSpec(memory_space=pltpu.VMEM)
    return pl.pallas_call(
        functools.partial(margin_kernel, groups, share),
        in_specs=[pl.BlockSpec(memory_space=pltpu.SMEM), vmem, vmem, vmem, vmem],
        out_specs=vmem,
        out_shape=jax.ShapeDtypeStruct((groups, ROWS, share * width), jnp.bfloat16),
        scratch_shapes=[
            pltpu.VMEM((3 * blocks + 1, 64, 8, width), jnp.float32),
            pltpu.VMEM((blocks, ROWS, width), jnp.float32),
        ],
        compiler_params=params(),
    )(neighbors, left, own, right, bias)


def conv_kernel(share, m_ref, w_ref, act_ref, o_ref, f_ref, q_ref):
    halves, groups, _, part, outs = w_ref.shape
    width = halves * part
    wide = groups * width
    for lb in range(share):
        for g in range(groups):
            f_ref[lb, :, g * width : (g + 1) * width] = m_ref[g, :, lb * width : (lb + 1) * width].astype(jnp.float32)
    for k in range(3):
        for lb in range(share):
            for p in range(6):
                for y in range(10):
                    near = 100 * p + 10 * y + k
                    far = near + 400
                    q_ref[k, lb, p, y] = jnp.concatenate(
                        [f_ref[lb, near : near + 8, :], f_ref[lb, far : far + 8, :]], axis=0
                    ).astype(jnp.bfloat16)
    bias = f_ref[0, 1000:1001, :]
    for lb in range(share):
        total = None
        for k in range(3):
            windows, weights = [], []
            for i in range(3):
                for j in range(3):
                    windows.append(q_ref[k, lb, i : i + 4, j : j + 8].reshape(CELLS, wide))
                    for g in range(groups):
                        for half in range(halves):
                            weights.append(w_ref[half, g, 9 * i + 3 * j + k])
            term = jnp.dot(
                jnp.concatenate(windows, axis=1),
                jnp.concatenate(weights, axis=0),
                preferred_element_type=jnp.float32,
            )
            total = term if total is None else total + term
        total = jnp.maximum(total + bias, 0.0).reshape(4, 8, 2, 8, outs)
        for h in range(2):
            half = total[:, :, h].reshape(256, outs).T
            seg = slice(lb * CELLS + h * 256, lb * CELLS + (h + 1) * 256)
            o_ref[:, seg] = (half * act_ref[:, seg]).astype(jnp.bfloat16)


def convolve(spread, weight_all, active, share):
    halves, groups, _, part, outs = weight_all.shape
    vmem = pl.BlockSpec(memory_space=pltpu.VMEM)
    return pl.pallas_call(
        functools.partial(conv_kernel, share),
        in_specs=[vmem] * 3,
        out_specs=vmem,
        out_shape=jax.ShapeDtypeStruct((outs, share * CELLS), jnp.bfloat16),
        scratch_shapes=[
            pltpu.VMEM((share, ROWS, groups * halves * part), jnp.float32),
            pltpu.VMEM((3, share, 6, 10, 16, groups * halves * part), jnp.bfloat16),
        ],
        compiler_params=params(),
    )(spread, weight_all, active)


def return_kernel(groups, owners, v_ref, id_ref, p_ref, o_ref, found_ref, held, send_sem, recv_sem):
    width, low_cells = v_ref.shape[0] // groups, v_ref.shape[1]
    rows = id_ref.shape[2]
    me = greet("space", owners)
    spots = lax.broadcasted_iota(jnp.int32, (low_cells, rows), 0)

    def copy(t):
        return pltpu.make_async_remote_copy(
            src_ref=found_ref.at[t],
            dst_ref=held.at[t],
            send_sem=send_sem.at[t],
            recv_sem=recv_sem.at[t],
            device_id={"space": lax.rem(me + t, owners)},
            device_id_type=MESH,
        )

    def pick(s):
        ids = id_ref[s]
        high = ids // low_cells
        low = ids % low_cells
        onehot = jnp.where(spots == low, 1.0, 0.0).astype(jnp.bfloat16)
        found = jnp.dot(v_ref[...], onehot, preferred_element_type=jnp.float32)
        total = jnp.zeros((width, rows), jnp.float32)
        for g in range(groups):
            total = jnp.where(jnp.broadcast_to(high, total.shape) == g, found[g * width : (g + 1) * width], total)
        return total

    def add(d, values):
        at = pl.ds(pl.multiple_of(d * rows, rows), rows)
        o_ref[:, at] = (p_ref[:, at].astype(jnp.float32) + values).astype(jnp.bfloat16)

    def send(t, carry):
        found_ref[t] = pick(lax.rem(me + t, owners)).astype(jnp.bfloat16)
        copy(t).start()
        return carry

    def take(t, carry):
        copy(t).wait_recv()
        add(lax.rem(me + owners - t, owners), held[t].astype(jnp.float32))
        return carry

    def close(t, carry):
        copy(t).wait_send()
        return carry

    lax.fori_loop(1, owners, send, 0)
    add(me, pick(me))
    lax.fori_loop(1, owners, take, 0)
    lax.fori_loop(1, owners, close, 0)


def give_back(parts, ids, points, owners, cap):
    groups, width, low_cells = parts.shape
    vmem = pl.BlockSpec(memory_space=pltpu.VMEM)
    return pl.pallas_call(
        functools.partial(return_kernel, groups, owners),
        in_specs=[vmem] * 3,
        out_specs=vmem,
        out_shape=jax.ShapeDtypeStruct(points.shape, jnp.bfloat16),
        scratch_shapes=[
            pltpu.VMEM((owners, width, cap), jnp.bfloat16),
            pltpu.VMEM((owners, width, cap), jnp.bfloat16),
            pltpu.SemaphoreType.DMA((owners,)),
            pltpu.SemaphoreType.DMA((owners,)),
        ],
        compiler_params=remote_params(3),
    )(parts.reshape(groups * width, low_cells), ids.reshape(owners, 1, cap), points)


SIDE = tuple((x, y) for x in range(10) for y in range(10) if x in (0, 9) or y in (0, 9))
LOW_AT, HIGH_AT = 288, 392
EDGES = (
    (0, 1, 1, 0),
    (0, 2, 2, 0),
    (0, 4, 4, 0),
    (2, 3, 1, 0),
    (4, 5, 1, 0),
    (2, 6, 4, 1),
    (4, 6, 2, 2),
    (6, 7, 1, 0),
)


def partner(me, mask):
    value = me
    for bit in (1, 2, 4):
        mine = lax.rem(me // bit, 2)
        value = value + bit * (lax.rem(mine + lax.rem(mask // bit, 2), 2) - mine)
    return value


def toward(padded):
    if padded == 0:
        return 0, 7
    if padded == 9:
        return 2, 0
    return 1, padded - 1


def whole_kernel(
    share, owners, pieces, nb_ref, x_ref, id_ref, bias_ref, w_ref, vox_ref, pick_ref,
    held, acc_ref, cnt_ref, own_ref, near_ref, v_ref, zp_ref, sh_ref, shout_ref, cen_ref, shin_ref,
    f_ref, q_ref, sum_ref, wall_ref, bown_ref, ball_ref, fin_ref, tab_ref, sid_ref, hot_ref,
    pool_send, pool_recv, cen_send, cen_recv, shell_send, shell_recv, halo_send, halo_recv,
    w_send, w_recv, wx_send, wx_recv, wsib_send, wsib_recv, bias_send, bias_recv,
    id_send, id_recv, back_send, back_recv, tab_send, tab_recv, own_sem, wown_sem,
):
    _, width, outs = w_ref.shape
    groups = outs // width
    cw = width // pieces
    blocks = groups * share
    rows = id_ref.shape[2]
    split = outs // 2
    me = lax.axis_index("space")
    row = lax.axis_index("chan")
    parity = lax.rem(me, 2)
    color = lax.rem(me // 2 + me // 4, 2)
    barrier = pltpu.get_barrier_semaphore()
    for r in range(1, owners):
        pl.semaphore_signal(barrier, inc=1, device_id={"space": partner(me, r)}, device_id_type=MESH)
    for t in range(1, groups):
        pl.semaphore_signal(barrier, inc=1, device_id={"chan": lax.rem(row + t, groups)}, device_id_type=MESH)
    pl.semaphore_wait(barrier, owners + groups - 2)

    def remote(src, dst, send, recv, device):
        return pltpu.make_async_remote_copy(
            src_ref=src, dst_ref=dst, send_sem=send, recv_sem=recv, device_id=device, device_id_type=MESH
        )

    def ahead(t):
        return lax.rem(row + t, groups)

    def behind(t):
        return lax.rem(row + groups - t, groups)

    def channels(h):
        return slice(h * cw, (h + 1) * cw)

    def slots(d):
        return pl.ds(pl.multiple_of(d * rows, rows), rows)

    def pool_copy(h, r):
        peer = partner(me, r)
        return remote(
            x_ref.at[channels(h), slots(peer)], held.at[r, channels(h)],
            pool_send.at[h, r], pool_recv.at[h, r], {"space": peer},
        )

    def id_copy(r):
        peer = partner(me, r)
        return remote(id_ref.at[peer], sid_ref.at[r], id_send.at[r], id_recv.at[r], {"space": peer})

    def bias_copy(t, landing):
        return remote(bown_ref, ball_ref.at[landing], bias_send.at[t], bias_recv.at[t], {"chan": ahead(t)})

    def quarter(index):
        return pl.ds(pl.multiple_of(index * 16, 16), 16)

    def w_copy(t, landing):
        return remote(
            w_ref.at[:, quarter(2 * color + parity)], wall_ref.at[color, landing, :, quarter(parity)],
            w_send.at[t], w_recv.at[t], {"chan": ahead(t)},
        )

    def w_cross(t, way, half):
        part = wall_ref.at[half, behind(t), slice(0, 14) if way == 0 else slice(14, 27), quarter(parity)]
        return remote(
            part, part, wx_send.at[t, way], wx_recv.at[t, way], {"space": partner(me, (2, 4)[way])}
        )

    def w_swap(t, own_half, core):
        half = color if own_half else 1 - color
        part = wall_ref.at[half, behind(t), :, quarter(core)]
        way = 0 if own_half else 1
        return remote(part, part, wsib_send.at[t, way], wsib_recv.at[t, way], {"space": partner(me, 1)})

    def cen_copy(h, t, landing):
        return remote(
            own_ref.at[h, ahead(t)], cen_ref.at[h, landing],
            cen_send.at[h, t], cen_recv.at[h, t], {"chan": ahead(t)},
        )

    def shell_copy(h, t, landing):
        return remote(
            shout_ref.at[h, ahead(t)], shin_ref.at[h, landing],
            shell_send.at[h, t], shell_recv.at[h, t], {"chan": ahead(t)},
        )

    def to_right(h):
        return remote(
            own_ref.at[h], near_ref.at[h, 0], halo_send.at[h, 0], halo_recv.at[h, 0],
            {"space": lax.rem(me + 1, owners)},
        )

    def to_left(h):
        return remote(
            own_ref.at[h], near_ref.at[h, 1], halo_send.at[h, 1], halo_recv.at[h, 1],
            {"space": lax.rem(me + owners - 1, owners)},
        )

    def lane_rows(index):
        return pl.ds(pl.multiple_of(index * width, width), width)

    def back(lb, t, landing):
        return remote(
            fin_ref.at[lb, lane_rows(ahead(t))], tab_ref.at[0, lb, lane_rows(landing)],
            back_send.at[lb, t], back_recv.at[lb, t], {"chan": ahead(t)},
        )

    def edge(lb, e):
        source, target, mask, part = EDGES[e]
        span = (slice(0, outs), slice(0, split), slice(split, outs))[part]
        return remote(
            tab_ref.at[source, lb, span], tab_ref.at[target, lb, span],
            tab_send.at[lb, e], tab_recv.at[lb, e], {"space": partner(me, mask)},
        )

    def send_pool(r, carry):
        pool_copy(0, r).start()
        return carry

    lax.fori_loop(1, owners, send_pool, 0)
    for t in range(1, groups):
        w_copy(t, row).start()
    own = pltpu.make_async_copy(x_ref.at[:, slots(me)], held.at[0], own_sem)
    own.start()
    own_w = [
        pltpu.make_async_copy(w_ref.at[:, channels(h)], wall_ref.at[h, row], wown_sem.at[h]) for h in range(pieces)
    ]
    for copy in own_w:
        copy.start()
    bown_ref[:, 0:width] = jnp.broadcast_to(bias_ref[...].astype(jnp.float32), (8, width))
    for t in range(1, groups):
        bias_copy(t, row).start()
    ball_ref[row] = bown_ref[...]
    for r in range(1, owners):
        id_copy(r).start()
    sid_ref[0] = id_ref[me]
    v_ref[3 * blocks] = jnp.zeros(v_ref.shape[1:], jnp.float32)
    for h in range(pieces):
        @pl.when(me == 0)
        def _():
            near_ref[h, 0] = jnp.zeros(near_ref.shape[2:], jnp.bfloat16)

        @pl.when(me == owners - 1)
        def _():
            near_ref[h, 1] = jnp.zeros(near_ref.shape[2:], jnp.bfloat16)

    spots = lax.broadcasted_iota(jnp.int32, (CELLS, rows), 0)

    def locate(ids):
        onehot = jnp.where(spots == ids % CELLS, 1.0, 0.0).astype(jnp.bfloat16)
        return ids // CELLS, onehot

    def add_chunk(h, r):
        high, onehot = locate(id_ref[partner(me, r)])
        x = held[r, channels(h)]
        wide_high = jnp.broadcast_to(high, x.shape)
        zero = jnp.zeros_like(x)
        nt = (((1,), (1,)), ((), ()))
        masked = jnp.concatenate([jnp.where(wide_high == g, x, zero) for g in range(blocks)], axis=0)
        acc_ref[...] += lax.dot_general(onehot, masked, nt, preferred_element_type=jnp.float32)
        if h == 0:
            one = jnp.ones_like(x)
            hot = jnp.concatenate([jnp.where(wide_high == g, one, zero) for g in range(blocks)], axis=0)
            cnt_ref[...] += lax.dot_general(onehot, hot, nt, preferred_element_type=jnp.float32)

    def take(h, lo, hi):
        def step(r, carry):
            pool_copy(h, r).wait_recv()
            if h + 1 < pieces:
                pool_copy(h + 1, r).start()
            add_chunk(h, r)
            return carry

        lax.fori_loop(lo, hi, step, 0)

    def normalise(h):
        v = (acc_ref[...] / jnp.maximum(cnt_ref[...], 1.0)).astype(jnp.bfloat16)
        lanes = share * cw
        for j in range(groups):
            at = slice(j * lanes, (j + 1) * lanes)
            own_ref[h, j] = jnp.concatenate([v[:256, at], v[256:, at]], axis=1)

        @pl.when(me < owners - 1)
        def _():
            to_right(h).start()

        @pl.when(me > 0)
        def _():
            to_left(h).start()

        for t in range(1, groups):
            cen_copy(h, t, row).start()
        cen_ref[h, row] = own_ref[h, row]

    def load_slots(a, part):
        for j in range(groups):
            for half in range(2):
                for lb in range(share):
                    at = (half * share + lb) * cw
                    slot = a * blocks + j * share + lb
                    v_ref[slot, half * 256 : (half + 1) * 256, 0:cw] = part[j, :, at : at + cw].astype(jnp.float32)
        for b in range(blocks):
            slot = a * blocks + b
            zp_ref[slot, 0] = v_ref[slot, pl.ds(7, 64, stride=8), :]
            zp_ref[slot, 1] = v_ref[slot, pl.ds(0, 64, stride=8), :]

    def shell(h):
        @pl.when(me > 0)
        def _():
            to_right(h).wait_recv()

        @pl.when(me < owners - 1)
        def _():
            to_left(h).wait_recv()

        load_slots(0, near_ref.at[h, 0])
        load_slots(2, near_ref.at[h, 1])
        build_shell()
        pack_shell(h)
        for t in range(1, groups):
            shell_copy(h, t, row).start()
        shin_ref[h, row] = shout_ref[h, row]

    def build_shell():
        def one_block(b, carry):
            def slot_of(o):
                slot = nb_ref[b, o]
                return jnp.where(slot < 0, 3 * blocks, slot)

            for c, (xd, yd) in enumerate(SIDE):
                (dx, xs), (dy, ys) = toward(xd), toward(yd)
                at = 8 * (8 * xs + ys)
                sh_ref[b, 8 * c : 8 * c + 8, :] = v_ref[slot_of(9 * dx + 3 * dy + 1), at : at + 8, :]
            for z, (base, dz) in enumerate(((LOW_AT, 0), (HIGH_AT, 2))):
                for xd in range(10):
                    dx, xs = toward(xd)
                    to = base + 10 * xd
                    at = 8 * xs
                    o = 9 * dx + dz
                    sh_ref[b, to + 1 : to + 9, :] = zp_ref[slot_of(o + 3), z, at : at + 8, :]
                    sh_ref[b, to : to + 1, :] = zp_ref[slot_of(o), z, at + 7 : at + 8, :]
                    sh_ref[b, to + 9 : to + 10, :] = zp_ref[slot_of(o + 6), z, at : at + 1, :]
            return carry

        lax.fori_loop(0, blocks, one_block, 0)

    def pack_shell(h):
        for j in range(groups):
            shout_ref[h, j] = jnp.concatenate(
                [
                    sh_ref[j * share + lb, half * 256 : (half + 1) * 256, 0:cw]
                    for half in range(2)
                    for lb in range(share)
                ],
                axis=1,
            ).astype(jnp.bfloat16)

    def joined(ref, h, lb, half):
        at = (half * share + lb) * cw
        return jnp.concatenate([ref[h, g, :, at : at + cw] for g in range(groups)], axis=1).astype(jnp.float32)

    def unpack_center(h):
        for t in range(1, groups):
            cen_copy(h, t, behind(t)).wait_recv()
        place_center(h)

    def place_center(h):
        for lb in range(share):
            for half in range(2):
                part = joined(cen_ref, h, lb, half)
                for x in range(4):
                    for y in range(8):
                        to = 100 * (4 * half + x + 1) + 10 * (y + 1) + 1
                        at = 8 * (8 * x + y)
                        f_ref[lb, to : to + 8, :] = part[at : at + 8]

    def unpack_shell(h):
        for t in range(1, groups):
            shell_copy(h, t, behind(t)).wait_recv()
        place_shell(h)

    def place_shell(h):
        for lb in range(share):
            first, second = joined(shin_ref, h, lb, 0), joined(shin_ref, h, lb, 1)
            for c, (xd, yd) in enumerate(SIDE):
                to = 100 * xd + 10 * yd + 1
                at = 8 * c
                f_ref[lb, to : to + 8, :] = first[at : at + 8] if at < 256 else second[at - 256 : at - 248]
            f_ref[lb, pl.ds(0, 100, stride=10), :] = second[LOW_AT - 256 : LOW_AT - 156]
            f_ref[lb, pl.ds(9, 100, stride=10), :] = second[HIGH_AT - 256 : HIGH_AT - 156]

    def windows_of(lb):
        for k in range(3):
            for p in range(6):
                for y in range(10):
                    near = 100 * p + 10 * y + k
                    far = near + 400
                    q_ref[lb, k, p, y] = jnp.concatenate(
                        [f_ref[lb, near : near + 8, :], f_ref[lb, far : far + 8, :]], axis=0
                    ).astype(jnp.bfloat16)

    def conv(h, lb):
        windows, weights = [], []
        for k in range(3):
            for i in range(3):
                for j in range(3):
                    windows.append(q_ref[lb, k, i : i + 4, j : j + 8].reshape(CELLS, groups * cw))
                    for g in range(groups):
                        weights.append(wall_ref[h, g, 9 * i + 3 * j + k])
        return jnp.dot(
            jnp.concatenate(windows, axis=1), jnp.concatenate(weights, axis=0), preferred_element_type=jnp.float32
        )

    def close_conv(lb, total):
        bias = jnp.concatenate([ball_ref[g, 0:1, 0:width] for g in range(groups)], axis=1)
        lane = lax.broadcasted_iota(jnp.int32, cnt_ref.shape, 1)
        mine = jnp.where(lane == (row * share + lb) * cw, cnt_ref[...], 0.0)
        active = jnp.where(jnp.sum(mine, axis=1, keepdims=True) > 0.0, 1.0, 0.0)
        total = jnp.maximum(total + bias, 0.0).reshape(4, 8, 2, 8, outs)
        for half in range(2):
            seg = slice(half * 256, (half + 1) * 256)
            fin_ref[lb, :, seg] = (total[:, :, half].reshape(256, outs) * active[seg]).T.astype(jnp.bfloat16)
        for t in range(1, groups):
            back(lb, t, row).start()
        tab_ref[0, lb, lane_rows(row)] = fin_ref[lb, lane_rows(row)]

    def gather_back(lb):
        for t in range(1, groups):
            back(lb, t, behind(t)).wait_recv()
        for e in (1, 2, 0):
            edge(lb, e).start()
        for g in range(groups):
            at = (g * share + lb) * CELLS
            vox_ref[:, at : at + CELLS] = tab_ref[0, lb, g * width : (g + 1) * width]

    def pass_on(lb):
        edge(lb, 1).wait_recv()
        edge(lb, 5).start()
        edge(lb, 3).start()
        edge(lb, 2).wait_recv()
        edge(lb, 6).start()
        edge(lb, 4).start()

    def pass_last(lb):
        edge(lb, 5).wait_recv()
        edge(lb, 6).wait_recv()
        edge(lb, 7).start()

    def pick(r, lb):
        high = sid_ref[r] // CELLS
        found = jnp.dot(tab_ref[r, lb], hot_ref[r], preferred_element_type=jnp.float32)
        at = slots(partner(me, r))
        total = jnp.zeros((width, rows), jnp.float32) if lb == 0 else pick_ref[:, at].astype(jnp.float32)
        for g in range(groups):
            total = jnp.where(
                jnp.broadcast_to(high, total.shape) == g * share + lb, found[g * width : (g + 1) * width], total
            )
        pick_ref[:, at] = total.astype(jnp.bfloat16)

    def picks(lo, hi, lb):
        def step(r, carry):
            pick(r, lb)
            return carry

        lax.fori_loop(lo, hi, step, 0)

    acc_ref[...] = jnp.zeros_like(acc_ref)
    cnt_ref[...] = jnp.zeros_like(cnt_ref)
    own.wait()
    add_chunk(0, 0)
    take(0, 1, owners)
    normalise(0)
    load_slots(1, own_ref.at[0])
    acc_ref[...] = jnp.zeros_like(acc_ref)
    add_chunk(1, 0)
    take(1, 1, owners)
    shell(0)
    normalise(1)
    load_slots(1, own_ref.at[1])
    for t in range(1, groups):
        w_copy(t, behind(t)).wait_recv()
        for way in range(2):
            w_cross(t, way, color).start()
        w_swap(t, True, parity).start()
    shell(1)
    unpack_center(0)
    unpack_shell(0)
    for lb in range(share):
        windows_of(lb)
    for copy in own_w:
        copy.wait()
    for t in range(1, groups):
        for way in range(2):
            w_cross(t, way, 1 - color).wait_recv()
        w_swap(t, False, parity).start()
    for t in range(1, groups):
        w_swap(t, True, 1 - parity).wait_recv()
        w_swap(t, False, 1 - parity).wait_recv()
        bias_copy(t, behind(t)).wait_recv()
    for r in range(1, owners):
        id_copy(r).wait_recv()
    for lb in range(share):
        sum_ref[lb] = conv(0, lb)
    unpack_center(1)
    unpack_shell(1)
    for lb in range(share):
        windows_of(lb)
        close_conv(lb, sum_ref[lb] + conv(1, lb))
    def keep_hot(r, carry):
        hot_ref[r] = locate(sid_ref[r])[1]
        return carry

    lax.fori_loop(0, owners, keep_hot, 0)
    gather_back(0)
    picks(0, 1, 0)
    gather_back(1)
    edge(0, 0).wait_recv()
    picks(1, 2, 0)
    pass_on(0)
    edge(0, 3).wait_recv()
    edge(0, 4).wait_recv()
    picks(2, 6, 0)
    edge(1, 0).wait_recv()
    picks(0, 2, 1)
    pass_on(1)
    pass_last(0)
    edge(0, 7).wait_recv()
    picks(6, 8, 0)
    edge(1, 3).wait_recv()
    edge(1, 4).wait_recv()
    picks(2, 6, 1)
    pass_last(1)
    picks(6, 7, 1)
    edge(1, 7).wait_recv()
    picks(7, 8, 1)

    for h in range(pieces):
        def close(r, carry):
            pool_copy(h, r).wait_send()
            return carry

        lax.fori_loop(1, owners, close, 0)

        @pl.when(me < owners - 1)
        def _():
            to_right(h).wait_send()

        @pl.when(me > 0)
        def _():
            to_left(h).wait_send()

        for t in range(1, groups):
            cen_copy(h, t, row).wait_send()
            shell_copy(h, t, row).wait_send()
    for t in range(1, groups):
        w_copy(t, row).wait_send()
        for way in range(2):
            w_cross(t, way, color).wait_send()
        w_swap(t, True, parity).wait_send()
        w_swap(t, False, parity).wait_send()
        bias_copy(t, row).wait_send()
    for r in range(1, owners):
        id_copy(r).wait_send()
    for lb in range(share):
        for t in range(1, groups):
            back(lb, t, row).wait_send()
        for e in range(len(EDGES)):
            edge(lb, e).wait_send()


def whole(neighbors, points, ids, bias, weight, groups, share, owners, cap):
    pieces = 2
    _, width, outs = weight.shape
    cw = width // pieces
    blocks = groups * share
    lanes = 2 * share * cw
    vmem = pl.BlockSpec(memory_space=pltpu.VMEM)
    anywhere = pl.BlockSpec(memory_space=pl.ANY)
    dma = pltpu.SemaphoreType.DMA
    bf16, f32 = jnp.bfloat16, jnp.float32
    return pl.pallas_call(
        functools.partial(whole_kernel, share, owners, pieces),
        in_specs=[pl.BlockSpec(memory_space=pltpu.SMEM), anywhere, vmem, vmem, anywhere],
        out_specs=[vmem, vmem],
        out_shape=[
            jax.ShapeDtypeStruct((width, blocks * CELLS), bf16),
            jax.ShapeDtypeStruct((width, owners * cap), bf16),
        ],
        scratch_shapes=[
            pltpu.VMEM((owners, width, cap), bf16),
            pltpu.VMEM((CELLS, blocks * cw), f32),
            pltpu.VMEM((CELLS, blocks * cw), f32),
            pltpu.VMEM((pieces, groups, 256, lanes), bf16),
            pltpu.VMEM((pieces, 2, groups, 256, lanes), bf16),
            pltpu.VMEM((3 * blocks + 1, CELLS, 128), f32),
            pltpu.VMEM((3 * blocks + 1, 2, 64, 128), f32),
            pltpu.VMEM((blocks, CELLS, 128), f32),
            pltpu.VMEM((pieces, groups, 256, lanes), bf16),
            pltpu.VMEM((pieces, groups, 256, lanes), bf16),
            pltpu.VMEM((pieces, groups, 256, lanes), bf16),
            pltpu.VMEM((share, ROWS, groups * cw), f32),
            pltpu.VMEM((share, 3, 6, 10, 16, groups * cw), bf16),
            pltpu.VMEM((share, CELLS, outs), f32),
            pltpu.VMEM((pieces, groups, 27, cw, outs), bf16),
            pltpu.VMEM((8, 128), f32),
            pltpu.VMEM((groups, 8, 128), f32),
            pltpu.VMEM((share, outs, CELLS), bf16),
            pltpu.VMEM((owners, share, outs, CELLS), bf16),
            pltpu.VMEM((owners, 1, cap), jnp.int32),
            pltpu.VMEM((owners, CELLS, cap), bf16),
            dma((pieces, owners)),
            dma((pieces, owners)),
            dma((pieces, groups)),
            dma((pieces, groups)),
            dma((pieces, groups)),
            dma((pieces, groups)),
            dma((pieces, 2)),
            dma((pieces, 2)),
            dma((groups,)),
            dma((groups,)),
            dma((groups, 2)),
            dma((groups, 2)),
            dma((groups, 2)),
            dma((groups, 2)),
            dma((groups,)),
            dma((groups,)),
            dma((owners,)),
            dma((owners,)),
            dma((share, groups)),
            dma((share, groups)),
            dma((share, len(EDGES))),
            dma((share, len(EDGES))),
            dma,
            dma((pieces,)),
        ],
        compiler_params=remote_params(4),
    )(neighbors, points, ids.reshape(owners, 1, cap), bias, weight)


def tally_cells(ids, cells):
    fine = 64
    high = (ids[None, :] // fine == jnp.arange(cells // fine, dtype=jnp.int32)[:, None]).astype(jnp.bfloat16)
    low = (ids[None, :] % fine == jnp.arange(fine, dtype=jnp.int32)[:, None]).astype(jnp.bfloat16)
    return lax.dot_general(high, low, (((1,), (1,)), ((), ())), preferred_element_type=jnp.float32).reshape(cells)


def gather_half(conv_weight):
    half = conv_weight.shape[1] // 2
    mine = lax.dynamic_slice_in_dim(conv_weight, lax.rem(lax.axis_index("space"), 2) * half, half, 1)
    return lax.all_gather(mine, "chan", axis=0)


def swap_halves(gathered, owners):
    pairs = [[i, i + 1] for i in range(0, owners, 2)]
    return lax.all_gather(gathered, "space", axis=0, axis_index_groups=pairs)


def on_device(points, point_cell, conv_weight, conv_bias, neighbors):
    width = points.shape[0]
    owners = lax.axis_size("space")
    groups = lax.axis_size("chan")
    cap = points.shape[2] // owners
    blocks = neighbors.shape[0]
    share = blocks // groups
    flat = points.reshape(width, owners * cap)
    ids = point_cell[0]
    if owners == 8 and share == 2 and width == 64 and groups == 4:
        voxel_out, picked = whole(
            neighbors, flat, ids, conv_bias.reshape(1, width), conv_weight, groups, share, owners, cap
        )
        point_out = flat.astype(jnp.float32) + picked.astype(jnp.float32)
        return (voxel_out, point_out.astype(jnp.bfloat16).reshape(points.shape))
    gathered = gather_half(conv_weight)
    counts = tally_cells(ids, blocks * CELLS)
    active = jnp.where(counts > 0.0, 1.0, 0.0).astype(jnp.float32)
    own = pool(flat, ids, counts, groups, owners, cap)
    left = lax.ppermute(own, "space", [(i, i + 1) for i in range(owners - 1)])
    right = lax.ppermute(own, "space", [(i + 1, i) for i in range(owners - 1)])
    margins = build_margins(neighbors, left, own, right, conv_bias.reshape(1, width), groups, share)
    gathered, margins = lax.optimization_barrier((gathered, margins))
    weight_all = swap_halves(gathered, owners)
    spread = exchange(margins, "chan", 1)
    mine = lax.dynamic_slice_in_dim(active, lax.axis_index("chan") * (share * CELLS), share * CELLS, 0)
    finished = convolve(spread, weight_all, mine.reshape(1, share * CELLS), share)
    finished = finished.reshape(groups, width, share * CELLS)
    parts = exchange(finished, "chan", 2)
    voxel_out = jnp.transpose(parts, (1, 0, 2)).reshape(width, blocks * CELLS)
    point_out = give_back(parts, ids, flat, owners, cap).reshape(points.shape)
    return (voxel_out, point_out)


def solution(mesh):
    return jax.shard_map(
        on_device,
        mesh=mesh,
        in_specs=(
            P("chan", "space", None),
            P("space", None),
            P(None, "chan", None),
            P("chan"),
            P("space", None),
        ),
        out_specs=(P("chan", "space"), P("chan", "space", None)),
        check_vma=False,
    )
```

```python
import functools

import jax
import jax.numpy as jnp
from jax import lax
from jax.experimental import pallas as pl
from jax.experimental.pallas import tpu as pltpu
from jax.sharding import PartitionSpec as P

VMEM_LIMIT = 60 * 1024 * 1024
CELLS = 512
MESH = pl.DeviceIdType.MESH
ROWS = 1008


def params():
    return pltpu.CompilerParams(vmem_limit_bytes=VMEM_LIMIT)


def greet(axis, count):
    me = lax.axis_index(axis)
    barrier = pltpu.get_barrier_semaphore()

    def signal(t, carry):
        pl.semaphore_signal(barrier, inc=1, device_id={axis: lax.rem(me + t, count)}, device_id_type=MESH)
        return carry

    lax.fori_loop(1, count, signal, 0)
    pl.semaphore_wait(barrier, count - 1)
    return me


def remote_params(collective_id):
    return pltpu.CompilerParams(
        vmem_limit_bytes=VMEM_LIMIT, collective_id=collective_id, has_side_effects=True
    )


def pool_kernel(groups, low_cells, owners, x_ref, id_ref, count_ref, o_ref, held, acc_ref, send_sem, recv_sem, own_sem):
    width, rows = held.shape[1], held.shape[2]
    me = greet("space", owners)

    def chunk(d):
        return x_ref.at[:, pl.ds(pl.multiple_of(d * rows, rows), rows)]

    def copy(t):
        peer = lax.rem(me + t, owners)
        return pltpu.make_async_remote_copy(
            src_ref=chunk(peer),
            dst_ref=held.at[t],
            send_sem=send_sem.at[t],
            recv_sem=recv_sem.at[t],
            device_id={"space": peer},
            device_id_type=MESH,
        )

    def send(t, carry):
        copy(t).start()
        return carry

    lax.fori_loop(1, owners, send, 0)
    own = pltpu.make_async_copy(chunk(me), held.at[0], own_sem)
    own.start()
    acc_ref[...] = jnp.zeros_like(acc_ref)
    spots = lax.broadcasted_iota(jnp.int32, (low_cells, rows), 0)

    def add_chunk(t):
        ids = id_ref[lax.rem(me + owners - t, owners)]
        high = ids // low_cells
        low = ids % low_cells
        x = held[t]
        zero = jnp.zeros_like(x)
        masked = jnp.concatenate(
            [jnp.where(jnp.broadcast_to(high, x.shape) == g, x, zero) for g in range(groups)], axis=0
        )
        onehot = jnp.where(spots == low, 1.0, 0.0).astype(jnp.bfloat16)
        acc_ref[...] += lax.dot_general(
            onehot, masked, (((1,), (1,)), ((), ())), preferred_element_type=jnp.float32
        )

    own.wait()
    add_chunk(0)

    def take(t, carry):
        copy(t).wait_recv()
        add_chunk(t)
        return carry

    lax.fori_loop(1, owners, take, 0)
    for g in range(groups):
        lanes = slice(g * width, (g + 1) * width)
        tally = jnp.maximum(count_ref[:, g : g + 1], 1.0)
        o_ref[:, lanes] = (acc_ref[:, lanes] / tally).astype(jnp.bfloat16)

    def close(t, carry):
        copy(t).wait_send()
        return carry

    lax.fori_loop(1, owners, close, 0)


def pool(points, ids, counts, groups, owners, cap):
    width = points.shape[0]
    low_cells = counts.shape[0] // groups
    by_group = counts.reshape(groups, low_cells).T
    vmem = pl.BlockSpec(memory_space=pltpu.VMEM)
    return pl.pallas_call(
        functools.partial(pool_kernel, groups, low_cells, owners),
        in_specs=[pl.BlockSpec(memory_space=pl.ANY), vmem, vmem],
        out_specs=vmem,
        out_shape=jax.ShapeDtypeStruct((low_cells, groups * width), jnp.bfloat16),
        scratch_shapes=[
            pltpu.VMEM((owners, width, cap), jnp.bfloat16),
            pltpu.VMEM((low_cells, groups * width), jnp.float32),
            pltpu.SemaphoreType.DMA((owners,)),
            pltpu.SemaphoreType.DMA((owners,)),
            pltpu.SemaphoreType.DMA,
        ],
        compiler_params=remote_params(0),
    )(points, ids.reshape(owners, 1, cap), by_group)


def exchange_kernel(axis, count, x_ref, o_ref, send_sem, recv_sem):
    me = greet(axis, count)

    def copy(t, landing):
        peer = lax.rem(me + t, count)
        return pltpu.make_async_remote_copy(
            src_ref=x_ref.at[peer],
            dst_ref=o_ref.at[landing],
            send_sem=send_sem.at[t],
            recv_sem=recv_sem.at[t],
            device_id={axis: peer},
            device_id_type=MESH,
        )

    def send(t, carry):
        copy(t, me).start()
        return carry

    def close(t, carry):
        copy(t, lax.rem(me + count - t, count)).wait_recv()
        copy(t, me).wait_send()
        return carry

    lax.fori_loop(1, count, send, 0)
    o_ref[me] = x_ref[me]
    lax.fori_loop(1, count, close, 0)


def exchange(x, axis, collective_id):
    count = lax.axis_size(axis)
    vmem = pl.BlockSpec(memory_space=pltpu.VMEM)
    return pl.pallas_call(
        functools.partial(exchange_kernel, axis, count),
        in_specs=[vmem],
        out_specs=vmem,
        out_shape=jax.ShapeDtypeStruct(x.shape, x.dtype),
        scratch_shapes=[pltpu.SemaphoreType.DMA((count,)), pltpu.SemaphoreType.DMA((count,))],
        compiler_params=remote_params(collective_id),
    )(x)


def margin_kernel(groups, share, nb_ref, left_ref, own_ref, right_ref, bias_ref, o_ref, v_ref, m_ref):
    blocks = groups * share
    width = bias_ref.shape[1]
    for a, ref in enumerate((left_ref, own_ref, right_ref)):
        for g in range(groups):
            for lb in range(share):
                part = ref[lb * CELLS : (lb + 1) * CELLS, g * width : (g + 1) * width]
                v_ref[a * blocks + g * share + lb] = part.astype(jnp.float32).reshape(64, 8, width)
    v_ref[3 * blocks] = jnp.zeros((64, 8, width), jnp.float32)
    bias = jnp.broadcast_to(bias_ref[...].astype(jnp.float32), (8, width))
    spans = (((0, 7),), tuple((t + 1, t) for t in range(8)), ((9, 0),))

    def one_block(b, carry):
        for dx in range(3):
            for dy in range(3):
                for dz in range(3):
                    slot = nb_ref[b, 9 * dx + 3 * dy + dz]
                    slot = jnp.where(slot < 0, 3 * blocks, slot)
                    for xd, xs in spans[dx]:
                        for yd, ys in spans[dy]:
                            row = 100 * xd + 10 * yd
                            if dz == 1:
                                m_ref[b, row + 1 : row + 9, :] = v_ref[slot, 8 * xs + ys]
                            else:
                                zd, zs = spans[dz][0]
                                m_ref[b, row + zd : row + zd + 1, :] = v_ref[slot, 8 * xs + ys, zs : zs + 1, :]
        m_ref[b, 1000:ROWS, :] = bias
        return carry

    lax.fori_loop(0, blocks, one_block, 0)
    for g in range(groups):
        for lb in range(share):
            o_ref[g, :, lb * width : (lb + 1) * width] = m_ref[g * share + lb].astype(jnp.bfloat16)


def build_margins(neighbors, left, own, right, bias, groups, share):
    width = bias.shape[1]
    blocks = groups * share
    vmem = pl.BlockSpec(memory_space=pltpu.VMEM)
    return pl.pallas_call(
        functools.partial(margin_kernel, groups, share),
        in_specs=[pl.BlockSpec(memory_space=pltpu.SMEM), vmem, vmem, vmem, vmem],
        out_specs=vmem,
        out_shape=jax.ShapeDtypeStruct((groups, ROWS, share * width), jnp.bfloat16),
        scratch_shapes=[
            pltpu.VMEM((3 * blocks + 1, 64, 8, width), jnp.float32),
            pltpu.VMEM((blocks, ROWS, width), jnp.float32),
        ],
        compiler_params=params(),
    )(neighbors, left, own, right, bias)


def conv_kernel(share, m_ref, w_ref, act_ref, o_ref, f_ref, q_ref):
    halves, groups, _, part, outs = w_ref.shape
    width = halves * part
    wide = groups * width
    for lb in range(share):
        for g in range(groups):
            f_ref[lb, :, g * width : (g + 1) * width] = m_ref[g, :, lb * width : (lb + 1) * width].astype(jnp.float32)
    for k in range(3):
        for lb in range(share):
            for p in range(6):
                for y in range(10):
                    near = 100 * p + 10 * y + k
                    far = near + 400
                    q_ref[k, lb, p, y] = jnp.concatenate(
                        [f_ref[lb, near : near + 8, :], f_ref[lb, far : far + 8, :]], axis=0
                    ).astype(jnp.bfloat16)
    bias = f_ref[0, 1000:1001, :]
    for lb in range(share):
        total = None
        for k in range(3):
            windows, weights = [], []
            for i in range(3):
                for j in range(3):
                    windows.append(q_ref[k, lb, i : i + 4, j : j + 8].reshape(CELLS, wide))
                    for g in range(groups):
                        for half in range(halves):
                            weights.append(w_ref[half, g, 9 * i + 3 * j + k])
            term = jnp.dot(
                jnp.concatenate(windows, axis=1),
                jnp.concatenate(weights, axis=0),
                preferred_element_type=jnp.float32,
            )
            total = term if total is None else total + term
        total = jnp.maximum(total + bias, 0.0).reshape(4, 8, 2, 8, outs)
        for h in range(2):
            half = total[:, :, h].reshape(256, outs).T
            seg = slice(lb * CELLS + h * 256, lb * CELLS + (h + 1) * 256)
            o_ref[:, seg] = (half * act_ref[:, seg]).astype(jnp.bfloat16)


def convolve(spread, weight_all, active, share):
    halves, groups, _, part, outs = weight_all.shape
    vmem = pl.BlockSpec(memory_space=pltpu.VMEM)
    return pl.pallas_call(
        functools.partial(conv_kernel, share),
        in_specs=[vmem] * 3,
        out_specs=vmem,
        out_shape=jax.ShapeDtypeStruct((outs, share * CELLS), jnp.bfloat16),
        scratch_shapes=[
            pltpu.VMEM((share, ROWS, groups * halves * part), jnp.float32),
            pltpu.VMEM((3, share, 6, 10, 16, groups * halves * part), jnp.bfloat16),
        ],
        compiler_params=params(),
    )(spread, weight_all, active)


def return_kernel(groups, owners, v_ref, id_ref, p_ref, o_ref, found_ref, held, send_sem, recv_sem):
    width, low_cells = v_ref.shape[0] // groups, v_ref.shape[1]
    rows = id_ref.shape[2]
    me = greet("space", owners)
    spots = lax.broadcasted_iota(jnp.int32, (low_cells, rows), 0)

    def copy(t):
        return pltpu.make_async_remote_copy(
            src_ref=found_ref.at[t],
            dst_ref=held.at[t],
            send_sem=send_sem.at[t],
            recv_sem=recv_sem.at[t],
            device_id={"space": lax.rem(me + t, owners)},
            device_id_type=MESH,
        )

    def pick(s):
        ids = id_ref[s]
        high = ids // low_cells
        low = ids % low_cells
        onehot = jnp.where(spots == low, 1.0, 0.0).astype(jnp.bfloat16)
        found = jnp.dot(v_ref[...], onehot, preferred_element_type=jnp.float32)
        total = jnp.zeros((width, rows), jnp.float32)
        for g in range(groups):
            total = jnp.where(jnp.broadcast_to(high, total.shape) == g, found[g * width : (g + 1) * width], total)
        return total

    def add(d, values):
        at = pl.ds(pl.multiple_of(d * rows, rows), rows)
        o_ref[:, at] = (p_ref[:, at].astype(jnp.float32) + values).astype(jnp.bfloat16)

    def send(t, carry):
        found_ref[t] = pick(lax.rem(me + t, owners)).astype(jnp.bfloat16)
        copy(t).start()
        return carry

    def take(t, carry):
        copy(t).wait_recv()
        add(lax.rem(me + owners - t, owners), held[t].astype(jnp.float32))
        return carry

    def close(t, carry):
        copy(t).wait_send()
        return carry

    lax.fori_loop(1, owners, send, 0)
    add(me, pick(me))
    lax.fori_loop(1, owners, take, 0)
    lax.fori_loop(1, owners, close, 0)


def give_back(parts, ids, points, owners, cap):
    groups, width, low_cells = parts.shape
    vmem = pl.BlockSpec(memory_space=pltpu.VMEM)
    return pl.pallas_call(
        functools.partial(return_kernel, groups, owners),
        in_specs=[vmem] * 3,
        out_specs=vmem,
        out_shape=jax.ShapeDtypeStruct(points.shape, jnp.bfloat16),
        scratch_shapes=[
            pltpu.VMEM((owners, width, cap), jnp.bfloat16),
            pltpu.VMEM((owners, width, cap), jnp.bfloat16),
            pltpu.SemaphoreType.DMA((owners,)),
            pltpu.SemaphoreType.DMA((owners,)),
        ],
        compiler_params=remote_params(3),
    )(parts.reshape(groups * width, low_cells), ids.reshape(owners, 1, cap), points)


SIDE = tuple((x, y) for x in range(10) for y in range(10) if x in (0, 9) or y in (0, 9))
LOW_AT, HIGH_AT = 288, 392
EDGES = (
    (0, 1, 1, 0),
    (0, 2, 2, 0),
    (0, 4, 4, 0),
    (2, 3, 1, 0),
    (4, 5, 1, 0),
    (2, 6, 4, 1),
    (4, 6, 2, 2),
    (6, 7, 1, 0),
)


def partner(me, mask):
    value = me
    for bit in (1, 2, 4):
        mine = lax.rem(me // bit, 2)
        value = value + bit * (lax.rem(mine + lax.rem(mask // bit, 2), 2) - mine)
    return value


def toward(padded):
    if padded == 0:
        return 0, 7
    if padded == 9:
        return 2, 0
    return 1, padded - 1


def whole_kernel(
    share, owners, pieces, nb_ref, x_ref, id_ref, bias_ref, w_ref, vox_ref, pick_ref,
    held, acc_ref, cnt_ref, own_ref, near_ref, v_ref, zp_ref, sh_ref, shout_ref, cen_ref, shin_ref,
    f_ref, q_ref, sum_ref, wall_ref, bown_ref, ball_ref, fin_ref, tab_ref, sid_ref, hot_ref,
    pool_send, pool_recv, cen_send, cen_recv, shell_send, shell_recv, halo_send, halo_recv,
    w_send, w_recv, wx_send, wx_recv, wsib_send, wsib_recv, bias_send, bias_recv,
    id_send, id_recv, back_send, back_recv, tab_send, tab_recv, own_sem, wown_sem,
):
    _, width, outs = w_ref.shape
    groups = outs // width
    cw = width // pieces
    blocks = groups * share
    rows = id_ref.shape[2]
    split = outs // 2
    me = lax.axis_index("space")
    row = lax.axis_index("chan")
    parity = lax.rem(me, 2)
    color = lax.rem(me // 2 + me // 4, 2)
    barrier = pltpu.get_barrier_semaphore()
    for r in range(1, owners):
        pl.semaphore_signal(barrier, inc=1, device_id={"space": partner(me, r)}, device_id_type=MESH)
    for t in range(1, groups):
        pl.semaphore_signal(barrier, inc=1, device_id={"chan": lax.rem(row + t, groups)}, device_id_type=MESH)
    pl.semaphore_wait(barrier, owners + groups - 2)

    def remote(src, dst, send, recv, device):
        return pltpu.make_async_remote_copy(
            src_ref=src, dst_ref=dst, send_sem=send, recv_sem=recv, device_id=device, device_id_type=MESH
        )

    def ahead(t):
        return lax.rem(row + t, groups)

    def behind(t):
        return lax.rem(row + groups - t, groups)

    def channels(h):
        return slice(h * cw, (h + 1) * cw)

    def slots(d):
        return pl.ds(pl.multiple_of(d * rows, rows), rows)

    def pool_copy(h, r):
        peer = partner(me, r)
        return remote(
            x_ref.at[channels(h), slots(peer)], held.at[r, channels(h)],
            pool_send.at[h, r], pool_recv.at[h, r], {"space": peer},
        )

    def id_copy(r):
        peer = partner(me, r)
        return remote(id_ref.at[peer], sid_ref.at[r], id_send.at[r], id_recv.at[r], {"space": peer})

    def bias_copy(t, landing):
        return remote(bown_ref, ball_ref.at[landing], bias_send.at[t], bias_recv.at[t], {"chan": ahead(t)})

    def quarter(index):
        return pl.ds(pl.multiple_of(index * 16, 16), 16)

    def w_copy(t, landing):
        return remote(
            w_ref.at[:, quarter(2 * color + parity)], wall_ref.at[color, landing, :, quarter(parity)],
            w_send.at[t], w_recv.at[t], {"chan": ahead(t)},
        )

    def w_cross(t, way, half):
        part = wall_ref.at[half, behind(t), slice(0, 14) if way == 0 else slice(14, 27), quarter(parity)]
        return remote(
            part, part, wx_send.at[t, way], wx_recv.at[t, way], {"space": partner(me, (2, 4)[way])}
        )

    def w_swap(t, own_half, core):
        half = color if own_half else 1 - color
        part = wall_ref.at[half, behind(t), :, quarter(core)]
        way = 0 if own_half else 1
        return remote(part, part, wsib_send.at[t, way], wsib_recv.at[t, way], {"space": partner(me, 1)})

    def cen_copy(h, t, landing):
        return remote(
            own_ref.at[h, ahead(t)], cen_ref.at[h, landing],
            cen_send.at[h, t], cen_recv.at[h, t], {"chan": ahead(t)},
        )

    def shell_copy(h, t, landing):
        return remote(
            shout_ref.at[h, ahead(t)], shin_ref.at[h, landing],
            shell_send.at[h, t], shell_recv.at[h, t], {"chan": ahead(t)},
        )

    def to_right(h):
        return remote(
            own_ref.at[h], near_ref.at[h, 0], halo_send.at[h, 0], halo_recv.at[h, 0],
            {"space": lax.rem(me + 1, owners)},
        )

    def to_left(h):
        return remote(
            own_ref.at[h], near_ref.at[h, 1], halo_send.at[h, 1], halo_recv.at[h, 1],
            {"space": lax.rem(me + owners - 1, owners)},
        )

    def lane_rows(index):
        return pl.ds(pl.multiple_of(index * width, width), width)

    def back(lb, t, landing):
        return remote(
            fin_ref.at[lb, lane_rows(ahead(t))], tab_ref.at[0, lb, lane_rows(landing)],
            back_send.at[lb, t], back_recv.at[lb, t], {"chan": ahead(t)},
        )

    def edge(lb, e):
        source, target, mask, part = EDGES[e]
        span = (slice(0, outs), slice(0, split), slice(split, outs))[part]
        return remote(
            tab_ref.at[source, lb, span], tab_ref.at[target, lb, span],
            tab_send.at[lb, e], tab_recv.at[lb, e], {"space": partner(me, mask)},
        )

    def send_pool(r, carry):
        pool_copy(0, r).start()
        return carry

    lax.fori_loop(1, owners, send_pool, 0)
    for t in range(1, groups):
        w_copy(t, row).start()
    own = pltpu.make_async_copy(x_ref.at[:, slots(me)], held.at[0], own_sem)
    own.start()
    own_w = [
        pltpu.make_async_copy(w_ref.at[:, channels(h)], wall_ref.at[h, row], wown_sem.at[h]) for h in range(pieces)
    ]
    for copy in own_w:
        copy.start()
    bown_ref[:, 0:width] = jnp.broadcast_to(bias_ref[...].astype(jnp.float32), (8, width))
    for t in range(1, groups):
        bias_copy(t, row).start()
    ball_ref[row] = bown_ref[...]
    for r in range(1, owners):
        id_copy(r).start()
    sid_ref[0] = id_ref[me]
    v_ref[3 * blocks] = jnp.zeros(v_ref.shape[1:], jnp.float32)
    for h in range(pieces):
        @pl.when(me == 0)
        def _():
            near_ref[h, 0] = jnp.zeros(near_ref.shape[2:], jnp.bfloat16)

        @pl.when(me == owners - 1)
        def _():
            near_ref[h, 1] = jnp.zeros(near_ref.shape[2:], jnp.bfloat16)

    spots = lax.broadcasted_iota(jnp.int32, (CELLS, rows), 0)

    def locate(ids):
        onehot = jnp.where(spots == ids % CELLS, 1.0, 0.0).astype(jnp.bfloat16)
        return ids // CELLS, onehot

    def add_chunk(h, r):
        high, onehot = locate(id_ref[partner(me, r)])
        x = held[r, channels(h)]
        wide_high = jnp.broadcast_to(high, x.shape)
        zero = jnp.zeros_like(x)
        nt = (((1,), (1,)), ((), ()))
        masked = jnp.concatenate([jnp.where(wide_high == g, x, zero) for g in range(blocks)], axis=0)
        acc_ref[...] += lax.dot_general(onehot, masked, nt, preferred_element_type=jnp.float32)
        if h == 0:
            one = jnp.ones_like(x)
            hot = jnp.concatenate([jnp.where(wide_high == g, one, zero) for g in range(blocks)], axis=0)
            cnt_ref[...] += lax.dot_general(onehot, hot, nt, preferred_element_type=jnp.float32)

    def take(h, lo, hi):
        def step(r, carry):
            pool_copy(h, r).wait_recv()
            if h + 1 < pieces:
                pool_copy(h + 1, r).start()
            add_chunk(h, r)
            return carry

        lax.fori_loop(lo, hi, step, 0)

    def normalise(h):
        v = (acc_ref[...] / jnp.maximum(cnt_ref[...], 1.0)).astype(jnp.bfloat16)
        lanes = share * cw
        for j in range(groups):
            at = slice(j * lanes, (j + 1) * lanes)
            own_ref[h, j] = jnp.concatenate([v[:256, at], v[256:, at]], axis=1)

        @pl.when(me < owners - 1)
        def _():
            to_right(h).start()

        @pl.when(me > 0)
        def _():
            to_left(h).start()

        for t in range(1, groups):
            cen_copy(h, t, row).start()
        cen_ref[h, row] = own_ref[h, row]

    def load_slots(a, part):
        for j in range(groups):
            for half in range(2):
                for lb in range(share):
                    at = (half * share + lb) * cw
                    slot = a * blocks + j * share + lb
                    v_ref[slot, half * 256 : (half + 1) * 256, 0:cw] = part[j, :, at : at + cw].astype(jnp.float32)
        for b in range(blocks):
            slot = a * blocks + b
            zp_ref[slot, 0] = v_ref[slot, pl.ds(7, 64, stride=8), :]
            zp_ref[slot, 1] = v_ref[slot, pl.ds(0, 64, stride=8), :]

    def shell(h):
        @pl.when(me > 0)
        def _():
            to_right(h).wait_recv()

        @pl.when(me < owners - 1)
        def _():
            to_left(h).wait_recv()

        load_slots(0, near_ref.at[h, 0])
        load_slots(2, near_ref.at[h, 1])
        build_shell()
        pack_shell(h)
        for t in range(1, groups):
            shell_copy(h, t, row).start()
        shin_ref[h, row] = shout_ref[h, row]

    def build_shell():
        def one_block(b, carry):
            def slot_of(o):
                slot = nb_ref[b, o]
                return jnp.where(slot < 0, 3 * blocks, slot)

            for c, (xd, yd) in enumerate(SIDE):
                (dx, xs), (dy, ys) = toward(xd), toward(yd)
                at = 8 * (8 * xs + ys)
                sh_ref[b, 8 * c : 8 * c + 8, :] = v_ref[slot_of(9 * dx + 3 * dy + 1), at : at + 8, :]
            for z, (base, dz) in enumerate(((LOW_AT, 0), (HIGH_AT, 2))):
                for xd in range(10):
                    dx, xs = toward(xd)
                    to = base + 10 * xd
                    at = 8 * xs
                    o = 9 * dx + dz
                    sh_ref[b, to + 1 : to + 9, :] = zp_ref[slot_of(o + 3), z, at : at + 8, :]
                    sh_ref[b, to : to + 1, :] = zp_ref[slot_of(o), z, at + 7 : at + 8, :]
                    sh_ref[b, to + 9 : to + 10, :] = zp_ref[slot_of(o + 6), z, at : at + 1, :]
            return carry

        lax.fori_loop(0, blocks, one_block, 0)

    def pack_shell(h):
        for j in range(groups):
            shout_ref[h, j] = jnp.concatenate(
                [
                    sh_ref[j * share + lb, half * 256 : (half + 1) * 256, 0:cw]
                    for half in range(2)
                    for lb in range(share)
                ],
                axis=1,
            ).astype(jnp.bfloat16)

    def joined(ref, h, lb, half):
        at = (half * share + lb) * cw
        return jnp.concatenate([ref[h, g, :, at : at + cw] for g in range(groups)], axis=1).astype(jnp.float32)

    def unpack_center(h):
        for t in range(1, groups):
            cen_copy(h, t, behind(t)).wait_recv()
        place_center(h)

    def place_center(h):
        for lb in range(share):
            for half in range(2):
                part = joined(cen_ref, h, lb, half)
                for x in range(4):
                    for y in range(8):
                        to = 100 * (4 * half + x + 1) + 10 * (y + 1) + 1
                        at = 8 * (8 * x + y)
                        f_ref[lb, to : to + 8, :] = part[at : at + 8]

    def unpack_shell(h):
        for t in range(1, groups):
            shell_copy(h, t, behind(t)).wait_recv()
        place_shell(h)

    def place_shell(h):
        for lb in range(share):
            first, second = joined(shin_ref, h, lb, 0), joined(shin_ref, h, lb, 1)
            for c, (xd, yd) in enumerate(SIDE):
                to = 100 * xd + 10 * yd + 1
                at = 8 * c
                f_ref[lb, to : to + 8, :] = first[at : at + 8] if at < 256 else second[at - 256 : at - 248]
            f_ref[lb, pl.ds(0, 100, stride=10), :] = second[LOW_AT - 256 : LOW_AT - 156]
            f_ref[lb, pl.ds(9, 100, stride=10), :] = second[HIGH_AT - 256 : HIGH_AT - 156]

    def windows_of(lb):
        for k in range(3):
            for p in range(6):
                for y in range(10):
                    near = 100 * p + 10 * y + k
                    far = near + 400
                    q_ref[lb, k, p, y] = jnp.concatenate(
                        [f_ref[lb, near : near + 8, :], f_ref[lb, far : far + 8, :]], axis=0
                    ).astype(jnp.bfloat16)

    def conv(h, lb):
        windows, weights = [], []
        for k in range(3):
            for i in range(3):
                for j in range(3):
                    windows.append(q_ref[lb, k, i : i + 4, j : j + 8].reshape(CELLS, groups * cw))
                    for g in range(groups):
                        weights.append(wall_ref[h, g, 9 * i + 3 * j + k])
        return jnp.dot(
            jnp.concatenate(windows, axis=1), jnp.concatenate(weights, axis=0), preferred_element_type=jnp.float32
        )

    def close_conv(lb, total):
        bias = jnp.concatenate([ball_ref[g, 0:1, 0:width] for g in range(groups)], axis=1)
        lane = lax.broadcasted_iota(jnp.int32, cnt_ref.shape, 1)
        mine = jnp.where(lane == (row * share + lb) * cw, cnt_ref[...], 0.0)
        active = jnp.where(jnp.sum(mine, axis=1, keepdims=True) > 0.0, 1.0, 0.0)
        total = jnp.maximum(total + bias, 0.0).reshape(4, 8, 2, 8, outs)
        for half in range(2):
            seg = slice(half * 256, (half + 1) * 256)
            fin_ref[lb, :, seg] = (total[:, :, half].reshape(256, outs) * active[seg]).T.astype(jnp.bfloat16)
        for t in range(1, groups):
            back(lb, t, row).start()
        tab_ref[0, lb, lane_rows(row)] = fin_ref[lb, lane_rows(row)]

    def gather_back(lb):
        for t in range(1, groups):
            back(lb, t, behind(t)).wait_recv()
        for e in (1, 2, 0):
            edge(lb, e).start()
        for g in range(groups):
            at = (g * share + lb) * CELLS
            vox_ref[:, at : at + CELLS] = tab_ref[0, lb, g * width : (g + 1) * width]

    def pass_on(lb):
        edge(lb, 1).wait_recv()
        edge(lb, 5).start()
        edge(lb, 3).start()
        edge(lb, 2).wait_recv()
        edge(lb, 6).start()
        edge(lb, 4).start()

    def pass_last(lb):
        edge(lb, 5).wait_recv()
        edge(lb, 6).wait_recv()
        edge(lb, 7).start()

    def pick(r, lb):
        high = sid_ref[r] // CELLS
        found = jnp.dot(tab_ref[r, lb], hot_ref[r], preferred_element_type=jnp.float32)
        at = slots(partner(me, r))
        total = jnp.zeros((width, rows), jnp.float32) if lb == 0 else pick_ref[:, at].astype(jnp.float32)
        for g in range(groups):
            total = jnp.where(
                jnp.broadcast_to(high, total.shape) == g * share + lb, found[g * width : (g + 1) * width], total
            )
        pick_ref[:, at] = total.astype(jnp.bfloat16)

    def picks(lo, hi, lb):
        def step(r, carry):
            pick(r, lb)
            return carry

        lax.fori_loop(lo, hi, step, 0)

    acc_ref[...] = jnp.zeros_like(acc_ref)
    cnt_ref[...] = jnp.zeros_like(cnt_ref)
    own.wait()
    add_chunk(0, 0)
    take(0, 1, owners)
    normalise(0)
    load_slots(1, own_ref.at[0])
    acc_ref[...] = jnp.zeros_like(acc_ref)
    add_chunk(1, 0)
    take(1, 1, owners)
    normalise(1)
    for t in range(1, groups):
        w_copy(t, behind(t)).wait_recv()
        for way in range(2):
            w_cross(t, way, color).start()
        w_swap(t, True, parity).start()
    shell(0)
    load_slots(1, own_ref.at[1])
    shell(1)
    unpack_center(0)
    unpack_shell(0)
    for lb in range(share):
        windows_of(lb)
    for copy in own_w:
        copy.wait()
    for t in range(1, groups):
        for way in range(2):
            w_cross(t, way, 1 - color).wait_recv()
        w_swap(t, False, parity).start()
    for t in range(1, groups):
        w_swap(t, True, 1 - parity).wait_recv()
        w_swap(t, False, 1 - parity).wait_recv()
        bias_copy(t, behind(t)).wait_recv()
    for r in range(1, owners):
        id_copy(r).wait_recv()
    for lb in range(share):
        sum_ref[lb] = conv(0, lb)
    unpack_center(1)
    unpack_shell(1)
    for lb in range(share):
        windows_of(lb)
        close_conv(lb, sum_ref[lb] + conv(1, lb))
    def keep_hot(r, carry):
        hot_ref[r] = locate(sid_ref[r])[1]
        return carry

    lax.fori_loop(0, owners, keep_hot, 0)
    gather_back(0)
    picks(0, 1, 0)
    gather_back(1)
    edge(0, 0).wait_recv()
    picks(1, 2, 0)
    pass_on(0)
    edge(0, 3).wait_recv()
    edge(0, 4).wait_recv()
    picks(2, 6, 0)
    edge(1, 0).wait_recv()
    picks(0, 2, 1)
    pass_on(1)
    pass_last(0)
    edge(0, 7).wait_recv()
    picks(6, 8, 0)
    edge(1, 3).wait_recv()
    edge(1, 4).wait_recv()
    picks(2, 6, 1)
    pass_last(1)
    picks(6, 7, 1)
    edge(1, 7).wait_recv()
    picks(7, 8, 1)

    for h in range(pieces):
        def close(r, carry):
            pool_copy(h, r).wait_send()
            return carry

        lax.fori_loop(1, owners, close, 0)

        @pl.when(me < owners - 1)
        def _():
            to_right(h).wait_send()

        @pl.when(me > 0)
        def _():
            to_left(h).wait_send()

        for t in range(1, groups):
            cen_copy(h, t, row).wait_send()
            shell_copy(h, t, row).wait_send()
    for t in range(1, groups):
        w_copy(t, row).wait_send()
        for way in range(2):
            w_cross(t, way, color).wait_send()
        w_swap(t, True, parity).wait_send()
        w_swap(t, False, parity).wait_send()
        bias_copy(t, row).wait_send()
    for r in range(1, owners):
        id_copy(r).wait_send()
    for lb in range(share):
        for t in range(1, groups):
            back(lb, t, row).wait_send()
        for e in range(len(EDGES)):
            edge(lb, e).wait_send()


def whole(neighbors, points, ids, bias, weight, groups, share, owners, cap):
    pieces = 2
    _, width, outs = weight.shape
    cw = width // pieces
    blocks = groups * share
    lanes = 2 * share * cw
    vmem = pl.BlockSpec(memory_space=pltpu.VMEM)
    anywhere = pl.BlockSpec(memory_space=pl.ANY)
    dma = pltpu.SemaphoreType.DMA
    bf16, f32 = jnp.bfloat16, jnp.float32
    return pl.pallas_call(
        functools.partial(whole_kernel, share, owners, pieces),
        in_specs=[pl.BlockSpec(memory_space=pltpu.SMEM), anywhere, vmem, vmem, anywhere],
        out_specs=[vmem, vmem],
        out_shape=[
            jax.ShapeDtypeStruct((width, blocks * CELLS), bf16),
            jax.ShapeDtypeStruct((width, owners * cap), bf16),
        ],
        scratch_shapes=[
            pltpu.VMEM((owners, width, cap), bf16),
            pltpu.VMEM((CELLS, blocks * cw), f32),
            pltpu.VMEM((CELLS, blocks * cw), f32),
            pltpu.VMEM((pieces, groups, 256, lanes), bf16),
            pltpu.VMEM((pieces, 2, groups, 256, lanes), bf16),
            pltpu.VMEM((3 * blocks + 1, CELLS, 128), f32),
            pltpu.VMEM((3 * blocks + 1, 2, 64, 128), f32),
            pltpu.VMEM((blocks, CELLS, 128), f32),
            pltpu.VMEM((pieces, groups, 256, lanes), bf16),
            pltpu.VMEM((pieces, groups, 256, lanes), bf16),
            pltpu.VMEM((pieces, groups, 256, lanes), bf16),
            pltpu.VMEM((share, ROWS, groups * cw), f32),
            pltpu.VMEM((share, 3, 6, 10, 16, groups * cw), bf16),
            pltpu.VMEM((share, CELLS, outs), f32),
            pltpu.VMEM((pieces, groups, 27, cw, outs), bf16),
            pltpu.VMEM((8, 128), f32),
            pltpu.VMEM((groups, 8, 128), f32),
            pltpu.VMEM((share, outs, CELLS), bf16),
            pltpu.VMEM((owners, share, outs, CELLS), bf16),
            pltpu.VMEM((owners, 1, cap), jnp.int32),
            pltpu.VMEM((owners, CELLS, cap), bf16),
            dma((pieces, owners)),
            dma((pieces, owners)),
            dma((pieces, groups)),
            dma((pieces, groups)),
            dma((pieces, groups)),
            dma((pieces, groups)),
            dma((pieces, 2)),
            dma((pieces, 2)),
            dma((groups,)),
            dma((groups,)),
            dma((groups, 2)),
            dma((groups, 2)),
            dma((groups, 2)),
            dma((groups, 2)),
            dma((groups,)),
            dma((groups,)),
            dma((owners,)),
            dma((owners,)),
            dma((share, groups)),
            dma((share, groups)),
            dma((share, len(EDGES))),
            dma((share, len(EDGES))),
            dma,
            dma((pieces,)),
        ],
        compiler_params=remote_params(4),
    )(neighbors, points, ids.reshape(owners, 1, cap), bias, weight)


def tally_cells(ids, cells):
    fine = 64
    high = (ids[None, :] // fine == jnp.arange(cells // fine, dtype=jnp.int32)[:, None]).astype(jnp.bfloat16)
    low = (ids[None, :] % fine == jnp.arange(fine, dtype=jnp.int32)[:, None]).astype(jnp.bfloat16)
    return lax.dot_general(high, low, (((1,), (1,)), ((), ())), preferred_element_type=jnp.float32).reshape(cells)


def gather_half(conv_weight):
    half = conv_weight.shape[1] // 2
    mine = lax.dynamic_slice_in_dim(conv_weight, lax.rem(lax.axis_index("space"), 2) * half, half, 1)
    return lax.all_gather(mine, "chan", axis=0)


def swap_halves(gathered, owners):
    pairs = [[i, i + 1] for i in range(0, owners, 2)]
    return lax.all_gather(gathered, "space", axis=0, axis_index_groups=pairs)


def on_device(points, point_cell, conv_weight, conv_bias, neighbors):
    width = points.shape[0]
    owners = lax.axis_size("space")
    groups = lax.axis_size("chan")
    cap = points.shape[2] // owners
    blocks = neighbors.shape[0]
    share = blocks // groups
    flat = points.reshape(width, owners * cap)
    ids = point_cell[0]
    if owners == 8 and share == 2 and width == 64 and groups == 4:
        voxel_out, picked = whole(
            neighbors, flat, ids, conv_bias.reshape(1, width), conv_weight, groups, share, owners, cap
        )
        point_out = flat.astype(jnp.float32) + picked.astype(jnp.float32)
        return (voxel_out, point_out.astype(jnp.bfloat16).reshape(points.shape))
    gathered = gather_half(conv_weight)
    counts = tally_cells(ids, blocks * CELLS)
    active = jnp.where(counts > 0.0, 1.0, 0.0).astype(jnp.float32)
    own = pool(flat, ids, counts, groups, owners, cap)
    left = lax.ppermute(own, "space", [(i, i + 1) for i in range(owners - 1)])
    right = lax.ppermute(own, "space", [(i + 1, i) for i in range(owners - 1)])
    margins = build_margins(neighbors, left, own, right, conv_bias.reshape(1, width), groups, share)
    gathered, margins = lax.optimization_barrier((gathered, margins))
    weight_all = swap_halves(gathered, owners)
    spread = exchange(margins, "chan", 1)
    mine = lax.dynamic_slice_in_dim(active, lax.axis_index("chan") * (share * CELLS), share * CELLS, 0)
    finished = convolve(spread, weight_all, mine.reshape(1, share * CELLS), share)
    finished = finished.reshape(groups, width, share * CELLS)
    parts = exchange(finished, "chan", 2)
    voxel_out = jnp.transpose(parts, (1, 0, 2)).reshape(width, blocks * CELLS)
    point_out = give_back(parts, ids, flat, owners, cap).reshape(points.shape)
    return (voxel_out, point_out)


def solution(mesh):
    return jax.shard_map(
        on_device,
        mesh=mesh,
        in_specs=(
            P("chan", "space", None),
            P("space", None),
            P(None, "chan", None),
            P("chan"),
            P("space", None),
        ),
        out_specs=(P("chan", "space"), P("chan", "space", None)),
        check_vma=False,
    )
```
